32 devices in a mesh: gx: 4 (over y, x), gy: 8 (over z, core).
Axes of the slice: x: 2, y: 2, z: 4, core: 2. Of those that a mesh axis runs over, the one named last changes fastest.
Arguments:
- material: int32 [8, 128, 512], P('gx', 'gy'), may hold values from 0 to 3
- phase: int32 [8, 128, 512], P('gx', 'gy'), may hold values from 0 to 7
- clock: float32 [1], replicated, may hold values from -3.140625 to 3.140625
- displacement: float32 [3, 8, 128, 512], P(None, 'gx', 'gy'), may hold values from -6 to 6
- velocity: float32 [3, 8, 128, 512], P(None, 'gx', 'gy'), may hold values from -6 to 6
- cotangent: float32 [3, 8, 128, 512], P(None, 'gx', 'gy'), may hold values from -4 to 4
- material_table: float32 [2, 4], replicated, may hold values from 0.5 to 4
- w_in: bfloat16 [256, 10], replicated, may hold values from -2 to 2
- b_in: float32 [256], replicated, may hold values from -3 to 3
- w_mid: bfloat16 [2, 256, 256], replicated, may hold values from -0.375 to 0.375
- b_mid: float32 [2, 256], replicated, may hold values from -3 to 3
- w_out: bfloat16 [9, 256], replicated, may hold values from -0.375 to 0.375
- b_out: float32 [9], replicated, may hold values from -3 to 3
Outputs:
- velocity_new: float32 [3, 8, 128, 512], P(None, 'gx', 'gy')
- displacement_grad: float32 [3, 8, 128, 512], P(None, 'gx', 'gy')
- grad_w_in: float32 [256, 10], replicated
- grad_b_in: float32 [256], replicated
- grad_w_mid: float32 [2, 256, 256], replicated
- grad_b_mid: float32 [2, 256], replicated
- grad_w_out: float32 [9, 256], replicated
- grad_b_out: float32 [9], replicated
The draws below stay inside these ranges and needn't reach their ends.
All inputs are finite; a program needn't handle non-finite values.
Results may differ from the reference program's by a relative error of at most 0.02.
Values sent between devices are 32-bit elements; how exact they have to be, the bound alone decides.
No kernel may reach another device: no remote copies, remote signals or barrier semaphores. Data moves between devices by JAX's collectives and lax.ppermute only.
A program may use at most 64 MiB of HBM per device.

```python
import math
import jax
import jax.numpy as jnp
from jax import lax

HID = 256
FEAT = 10
OUT = 9
MATS = 4
PHASES = 8
NX = 8
NY = 128
NZ = 512
NPARAM = 136713


def draw_cotangent(key, part):
    shape = (3, NX, NY, NZ)
    return jnp.clip(jax.random.normal(key, shape, jnp.float32), -4.0, 4.0)


def touch_ends(entries, key, least, high):
    index_at = [jax.random.randint(jax.random.fold_in(key, axis), (), 0, length) for axis, length in enumerate(entries.shape)]
    longest = entries.shape.index(max(entries.shape))
    neighbour = index_at[:longest] + [(index_at[longest] + 1) % entries.shape[longest]] + index_at[longest + 1:]
    return entries.at[tuple(index_at)].set(least).at[tuple(neighbour)].set(high)


def levels(own_key, shape, cuts, low, top_value):
    level, own = 1.0, jax.random.fold_in(own_key, 6)
    for dim, parts in cuts:
        steps = jnp.exp(jax.random.uniform(jax.random.fold_in(own, dim), (parts,), jnp.float32, low / len(cuts), top_value / len(cuts)))
        level = level * jnp.repeat(steps, shape[dim] // parts).reshape([-1 if axis == dim else 1 for axis in range(len(shape))])
    return level


def bell_draw(key, extent, scale, most, cuts=(), kind=jnp.bfloat16):
    factor_of = levels(key, extent, cuts, -0.22, 0.18) if cuts else 1.0
    values = jax.random.normal(key, extent, jnp.float32) * scale * factor_of
    return jnp.minimum(jnp.maximum(values, -most), most).astype(kind)


def setup_inputs(seed: int = 0) -> dict:
    splits = jax.random.split(jax.random.key(seed), 14)
    return {
        "material": touch_ends(jax.random.randint(splits[0], (NX, NY, NZ), 0, MATS), jax.random.fold_in(splits[0], 1), 0, MATS - 1).astype(jnp.int32),
        "phase": touch_ends(jax.random.randint(splits[1], (NX, NY, NZ), 0, PHASES), jax.random.fold_in(splits[1], 1), 0, PHASES - 1).astype(jnp.int32),
        "clock": jnp.clip(jax.random.uniform(splits[2], (1,), jnp.float32, -3.140625, 3.140625), -3.140625, 3.140625),
        "displacement": bell_draw(splits[3], (3, NX, NY, NZ), 1.0, 6.0, ((1, 4), (2, 8)), jnp.float32),
        "velocity": bell_draw(splits[4], (3, NX, NY, NZ), 1.0, 6.0, ((1, 4), (2, 8)), jnp.float32),
        "cotangent": draw_cotangent(jax.random.fold_in(splits[13], 71), 0),
        "material_table": jnp.clip(jnp.exp(jax.random.uniform(splits[6], (2, MATS), jnp.float32, math.log(0.5), math.log(4.0))), 0.5, 4.0),
        "w_in": bell_draw(splits[7], (HID, FEAT), FEAT ** -0.5, 2.0),
        "b_in": bell_draw(splits[8], (HID,), 0.5, 3.0, (), jnp.float32),
        "w_mid": bell_draw(splits[9], (2, HID, HID), HID ** -0.5, 0.375),
        "b_mid": bell_draw(splits[10], (2, HID), 0.5, 3.0, (), jnp.float32),
        "w_out": bell_draw(splits[11], (OUT, HID), HID ** -0.5, 0.375),
        "b_out": bell_draw(splits[12], (OUT,), 0.5, 3.0, (), jnp.float32),
    }


time_step = 0.25
viscosity = 0.2
norm_eps = 1e-06
two_pi = 6.283185307179586

def central(field, axis):
    widths = [(0, 0)] * field.ndim
    widths[axis] = (1, 1)
    padded = jnp.pad(field, widths)
    length = field.shape[axis]
    return (lax.slice_in_dim(padded, 2, length + 2, axis=axis) - lax.slice_in_dim(padded, 0, length, axis=axis)) * 0.5

def laplace(field):
    total = -6.0 * field
    for axis in (1, 2, 3):
        widths = [(0, 0)] * field.ndim
        widths[axis] = (1, 1)
        padded = jnp.pad(field, widths)
        length = field.shape[axis]
        total = total + lax.slice_in_dim(padded, 2, length + 2, axis=axis) + lax.slice_in_dim(padded, 0, length, axis=axis)
    return total

def forward_block(feats, w_in, b_in, w_mid, b_mid, w_out, b_out):
    first = jnp.tanh(jnp.dot(w_in, feats, preferred_element_type=jnp.float32) + b_in[:, None]).astype(jnp.bfloat16)
    second = jnp.tanh(jnp.dot(w_mid[0], first, preferred_element_type=jnp.float32) + b_mid[0][:, None]).astype(jnp.bfloat16)
    third = jnp.tanh(jnp.dot(w_mid[1], second, preferred_element_type=jnp.float32) + b_mid[1][:, None]).astype(jnp.bfloat16)
    result = jnp.dot(w_out, third, preferred_element_type=jnp.float32) + b_out[:, None]
    return (first, second, third, result)

def backward_block(feats, delta, w_in, b_in, w_mid, b_mid, w_out, b_out):
    first, second, third, unused = forward_block(feats, w_in, b_in, w_mid, b_mid, w_out, b_out)
    delta_out = delta.astype(jnp.bfloat16)
    grad_wout = jnp.dot(delta_out, third.T, preferred_element_type=jnp.float32)
    grad_bout = lax.optimization_barrier(jnp.sum(delta_out.astype(jnp.float32), axis=1))
    back_third = jnp.dot(w_out.T, delta_out, preferred_element_type=jnp.float32)
    delta_third = (back_third * (1.0 - jnp.square(third.astype(jnp.float32)))).astype(jnp.bfloat16)
    grad_wthree = jnp.dot(delta_third, second.T, preferred_element_type=jnp.float32)
    grad_bthree = lax.optimization_barrier(jnp.sum(delta_third.astype(jnp.float32), axis=1))
    back_second = jnp.dot(w_mid[1].T, delta_third, preferred_element_type=jnp.float32)
    delta_second = (back_second * (1.0 - jnp.square(second.astype(jnp.float32)))).astype(jnp.bfloat16)
    grad_wtwo = jnp.dot(delta_second, first.T, preferred_element_type=jnp.float32)
    grad_btwo = lax.optimization_barrier(jnp.sum(delta_second.astype(jnp.float32), axis=1))
    back_first = jnp.dot(w_mid[0].T, delta_second, preferred_element_type=jnp.float32)
    delta_first = (back_first * (1.0 - jnp.square(first.astype(jnp.float32)))).astype(jnp.bfloat16)
    grad_win = jnp.dot(delta_first, feats.T, preferred_element_type=jnp.float32)
    grad_bin = lax.optimization_barrier(jnp.sum(delta_first.astype(jnp.float32), axis=1))
    back_feats = jnp.dot(w_in.T, delta_first, preferred_element_type=jnp.float32)
    grads = (grad_win, grad_bin, jnp.stack([grad_wtwo, grad_wthree]), jnp.stack([grad_btwo, grad_bthree]), grad_wout, grad_bout)
    return (grads, back_feats)

def reference(material, phase, clock, displacement, velocity, cotangent, material_table, w_in, b_in, w_mid, b_mid, w_out, b_out):
    kinds = jnp.arange(MATS, dtype=jnp.int32)
    onehot = (material[None] == kinds[:, None, None, None]).astype(jnp.float32)
    stiffness = jnp.tensordot(material_table[0], onehot, axes=1)
    density = jnp.tensordot(material_table[1], onehot, axes=1)
    occupied = (material > 0).astype(jnp.float32)
    actuation = jnp.sin(two_pi * phase.astype(jnp.float32) / PHASES + clock[0])
    strain = jnp.stack([central(displacement, 1), central(displacement, 2), central(displacement, 3)], axis=1).reshape(9, NX, NY, NZ)
    feats = jnp.concatenate([strain, actuation[None]], 0).reshape(FEAT, -1).astype(jnp.bfloat16)
    voxels = NX * NY * NZ
    block_rows = min(2048, voxels)
    count = voxels // block_rows
    feat_blocks = feats.reshape(FEAT, count, block_rows).transpose(1, 0, 2)
    weights = (w_in, b_in, w_mid, b_mid, w_out, b_out)
    outputs = lax.map(lambda piece: forward_block(piece, *weights)[3], feat_blocks)
    network = outputs.transpose(1, 0, 2).reshape(OUT, NX, NY, NZ)
    stress = (occupied * stiffness * network).reshape(3, 3, NX, NY, NZ)
    force = central(stress[:, 0], 1) + central(stress[:, 1], 2) + central(stress[:, 2], 3)
    velocity_new = velocity + time_step * occupied * (force + viscosity * laplace(velocity)) / density
    carried = time_step * occupied * cotangent / density
    stress_grad = -jnp.stack([central(carried, 1), central(carried, 2), central(carried, 3)], axis=1).reshape(9, NX, NY, NZ)
    delta_all = (occupied * stiffness * stress_grad).reshape(OUT, count, block_rows).transpose(1, 0, 2)
    zeros = (jnp.zeros(w_in.shape, jnp.float32), jnp.zeros(b_in.shape, jnp.float32), jnp.zeros(w_mid.shape, jnp.float32), jnp.zeros(b_mid.shape, jnp.float32), jnp.zeros(w_out.shape, jnp.float32), jnp.zeros(b_out.shape, jnp.float32))

    def step(carry, pieces):
        grads, back_feats = backward_block(pieces[0], pieces[1], *weights)
        return (jax.tree.map(lambda left, right: left + right, carry, grads), back_feats[:9])
    sums, back_blocks = lax.scan(step, zeros, (feat_blocks, delta_all))
    strain_grad = back_blocks.transpose(1, 0, 2).reshape(3, 3, NX, NY, NZ)
    displacement_grad = -(central(strain_grad[:, 0], 1) + central(strain_grad[:, 1], 2) + central(strain_grad[:, 2], 3))
    total = sum((jnp.sum(jnp.square(item)) for item in sums))
    scale = lax.rsqrt(total / NPARAM + norm_eps)
    return (velocity_new, displacement_grad, sums[0] * scale, sums[1] * scale, sums[2] * scale, sums[3] * scale, sums[4] * scale, sums[5] * scale)
```

```python
import functools
import jax
import jax.numpy as jnp
from jax import lax
from jax.experimental import pallas as pl
from jax.experimental.pallas import tpu as pltpu
from jax.sharding import PartitionSpec as P

FEAT = 10
OUT = 9
HID = 256
PHASES = 8
NPARAM = 136713
SMALL = 8
GROUPS = 5

time_step = 0.25
viscosity = 0.2
norm_eps = 1e-06
two_pi = 6.283185307179586

bf16 = jnp.bfloat16
f32 = jnp.float32
VMEM = pl.BlockSpec(memory_space=pltpu.VMEM)
SMEM = pl.BlockSpec(memory_space=pltpu.SMEM)


def pick(table, row, material):
    value = jnp.full(material.shape, table[row, 0], f32)
    for kind in range(1, table.shape[1]):
        value = jnp.where(material == kind, table[row, kind], value)
    return value


def step_factor(table, material):
    occupied = jnp.where(material > 0, 1.0, 0.0).astype(f32)
    return occupied, pick(table, 1, material)


def x_ends(field, low, high, rows):
    return (
        jnp.concatenate([low, field[:-rows]], 0),
        jnp.concatenate([field[rows:], high], 0),
    )


def y_ends(field, low, high, rows):
    planes = field.shape[0] // rows
    where = lax.broadcasted_iota(jnp.int32, field.shape, 0)

    def spread(edge):
        return jnp.concatenate(
            [jnp.broadcast_to(edge[p : p + 1], (rows, field.shape[1])) for p in range(planes)], 0
        )

    before, after = pltpu.roll(field, 1, 0), pltpu.roll(field, field.shape[0] - 1, 0)
    low = 0.0 if low is None else spread(low)
    high = 0.0 if high is None else spread(high)
    return (
        jnp.where(where % rows == 0, low, before),
        jnp.where(where % rows == rows - 1, high, after),
    )


def z_ends(field):
    lanes = field.shape[1]
    where = lax.broadcasted_iota(jnp.int32, field.shape, 1)
    return (
        jnp.where(where == 0, 0.0, pltpu.roll(field, 1, 1)),
        jnp.where(where == lanes - 1, 0.0, pltpu.roll(field, lanes - 1, 1)),
    )


def half_diff(ends):
    return (ends[1] - ends[0]) * 0.5


def faces_kernel(rows, table, material, displacement, velocity, cotangent, xf, xb, yf, yb, vf, vb):
    size = material.shape[0]
    planes = size // rows
    occupied, density = step_factor(table, material[...])
    for i in range(3):
        carried = time_step * occupied * cotangent[i] / density
        for slot, field in ((i, displacement[i]), (3 + i, carried), (6 + i, velocity[i])):
            if slot < 6:
                xf[slot] = field[size - rows :]
                xb[slot] = field[:rows]
            else:
                vf[i] = field[size - rows :]
                vb[i] = field[:rows]
            for p in range(planes):
                yf[slot, p : p + 1] = field[(p + 1) * rows - 1 : (p + 1) * rows]
                yb[slot, p : p + 1] = field[p * rows : p * rows + 1]


def network_kernel(
    rows,
    block,
    table,
    clock,
    b_out,
    material,
    phase,
    displacement,
    cotangent,
    xl,
    xh,
    yl,
    yh,
    w_in,
    b_in,
    w_mid,
    b_mid,
    w_out,
    sxf,
    sxb,
    syf,
    syb,
    force,
    dgrad,
    grads,
    grid_in,
    grid_delta,
    feats,
    delta,
    net,
    back,
    win,
    winT,
    wmidT,
    wout,
    woutT,
    bias,
    acc_mid,
    acc_in,
    acc_out,
    acc_b,
    acc_bo,
    tall,
    wide,
):
    size, lanes = material.shape
    planes = size // rows
    tiles = lanes // 128
    voxels = size * lanes
    mat = material[...]
    occupied, density = step_factor(table, mat)
    strength = occupied * pick(table, 0, mat)

    tall[...] = jnp.zeros_like(tall)
    tall[:, :FEAT] = w_in[...].astype(f32)
    win[...] = tall[:, :16].astype(bf16)
    winT[...] = tall[...].T[:16].astype(bf16)
    wide[...] = jnp.zeros_like(wide)
    wide[:OUT] = w_out[...].astype(f32)
    wout[...] = wide[:16].astype(bf16)
    woutT[...] = wide[...].T[:, :16].astype(bf16)
    for k in range(2):
        wmidT[k] = w_mid[k].astype(f32).T.astype(bf16)
    for k, row in enumerate((b_in[...], b_mid[0:1], b_mid[1:2])):
        bias[k] = jnp.broadcast_to(row, (128, HID)).T
    for ref in (acc_mid, acc_in, acc_out, acc_b, acc_bo):
        ref[...] = jnp.zeros_like(ref)

    def put(ref, slot, field):
        for t in range(tiles):
            ref[t, slot * size : (slot + 1) * size] = field[:, t * 128 : (t + 1) * 128]

    factor = time_step * occupied
    for i in range(3):
        field = displacement[i]
        put(grid_in, 3 * i, half_diff(x_ends(field, xl[i], xh[i], rows)))
        put(grid_in, 3 * i + 1, half_diff(y_ends(field, yl[i], yh[i], rows)))
        put(grid_in, 3 * i + 2, half_diff(z_ends(field)))
        field = factor * cotangent[i] / density
        put(grid_delta, 3 * i, strength * -half_diff(x_ends(field, xl[3 + i], xh[3 + i], rows)))
        put(grid_delta, 3 * i + 1, strength * -half_diff(y_ends(field, yl[3 + i], yh[3 + i], rows)))
        put(grid_delta, 3 * i + 2, strength * -half_diff(z_ends(field)))
    put(grid_in, 9, jnp.sin(two_pi * phase[...].astype(f32) / PHASES + clock[0]))
    put(grid_in, 10, jnp.ones((size, lanes), f32))
    for slot in range(11, 16):
        put(grid_in, slot, jnp.zeros((size, lanes), f32))
    for slot in range(9, 16):
        put(grid_delta, slot, jnp.zeros((size, lanes), f32))
    for r in range(size):
        for t in range(tiles):
            at = slice((r * tiles + t) * 128, (r * tiles + t + 1) * 128)
            feats[:, at] = grid_in[t, pl.ds(r, 16, stride=size), :].astype(bf16)
            delta[:, at] = grid_delta[t, pl.ds(r, 16, stride=size), :].astype(bf16)

    rowid = lax.broadcasted_iota(jnp.int32, (16, 1), 0)
    bias_out = jnp.zeros((16, 1), f32)
    for k in range(OUT):
        bias_out = jnp.where(rowid == k, b_out[k], bias_out)

    def mul(a, b):
        return jnp.dot(a, b, preferred_element_type=f32)

    def mul_t(a, b):
        return lax.dot_general(a, b, (((1,), (1,)), ((), ())), preferred_element_type=f32)

    def lane_sum(value):
        total = value[:, :128].astype(f32)
        for k in range(1, block // 128):
            total = total + value[:, k * 128 : (k + 1) * 128].astype(f32)
        return total

    def slope(value):
        wider = value.astype(f32)
        return 1.0 - wider * wider

    def step(index, carry):
        at = pl.ds(pl.multiple_of(index * block, block), block)
        f, d = feats[:, at], delta[:, at]
        h1 = jnp.tanh(mul(win[...], f) + bias[0][:, :1]).astype(bf16)
        h2 = jnp.tanh(mul(w_mid[0], h1) + bias[1][:, :1]).astype(bf16)
        h3 = jnp.tanh(mul(w_mid[1], h2) + bias[2][:, :1]).astype(bf16)
        net[:, at] = mul(wout[...], h3) + bias_out
        acc_out[...] += mul_t(d, h3)
        acc_bo[...] += lane_sum(d)
        d3 = (mul(woutT[...], d) * slope(h3)).astype(bf16)
        acc_mid[HID:] += mul_t(d3, h2)
        acc_b[1] += lane_sum(d3)
        d2 = (mul(wmidT[1], d3) * slope(h2)).astype(bf16)
        acc_mid[:HID] += mul_t(d2, h1)
        acc_b[0] += lane_sum(d2)
        d1 = (mul(wmidT[0], d2) * slope(h1)).astype(bf16)
        acc_in[...] += mul_t(f, d1)
        back[:, at] = mul(winT[...], d1)
        return carry

    lax.fori_loop(0, voxels // block, step, 0)

    for r in range(size):
        for t in range(tiles):
            at = slice((r * tiles + t) * 128, (r * tiles + t + 1) * 128)
            grid_in[t, pl.ds(r, 16, stride=size), :] = net[:, at]
            grid_delta[t, pl.ds(r, 16, stride=size), :] = back[:, at]

    def get(ref, slot):
        return jnp.concatenate(
            [ref[t, slot * size : (slot + 1) * size] for t in range(tiles)], axis=1
        )

    nothing = jnp.zeros((rows, lanes), f32)
    for base, ref, scale, out in ((0, grid_in, strength, force), (3, grid_delta, None, dgrad)):
        for i in range(3):
            along = [get(ref, 3 * i + j) for j in range(3)]
            if scale is not None:
                along = [scale * item for item in along]
            slot = base + i
            sxf[slot] = along[0][size - rows :]
            sxb[slot] = along[0][:rows]
            for p in range(planes):
                syf[slot, p : p + 1] = along[1][(p + 1) * rows - 1 : (p + 1) * rows]
                syb[slot, p : p + 1] = along[1][p * rows : p * rows + 1]
            out[i] = (
                half_diff(x_ends(along[0], nothing, nothing, rows))
                + half_diff(y_ends(along[1], None, None, rows))
                + half_diff(z_ends(along[2]))
            )

    chunks = grads.shape[0]
    part = 2 * HID // chunks
    for c in range(chunks):
        grads[c, :part] = acc_mid[c * part : (c + 1) * part]
        grads[c, part:] = jnp.zeros((SMALL, HID), f32)
    grads[0, part:] = acc_in[:8]
    grads[1, part:] = jnp.where(rowid[:8] < 3, acc_in[8:], 0.0)
    grads[2, part:] = acc_out[:8]
    grads[3, part:] = acc_out[8:]
    for k in range(2):
        grads[4, part + k : part + k + 1] = jnp.sum(acc_b[k].T, axis=0, keepdims=True)
    wide[...] = jnp.zeros_like(wide)
    wide[:16, :128] = acc_bo[...]
    grads[4, part + 2 : part + 3, :128] = jnp.sum(wide[:, :128].T, axis=0, keepdims=True)


def fields_kernel(
    rows,
    table,
    material,
    velocity,
    force,
    dgrad,
    vl,
    vh,
    yl,
    yh,
    sxl,
    sxh,
    syl,
    syh,
    velocity_new,
    displacement_grad,
):
    size, lanes = material.shape
    planes = size // rows
    occupied, density = step_factor(table, material[...])

    def halo_part(slot):
        middle = [jnp.zeros((rows, lanes), f32)] * (planes - 2)
        first, last = -0.5 * sxl[slot], 0.5 * sxh[slot]
        part = jnp.concatenate([first, *middle, last] if planes > 1 else [first + last], 0)
        where = lax.broadcasted_iota(jnp.int32, (size, lanes), 0)

        def spread(edge):
            return jnp.concatenate(
                [jnp.broadcast_to(edge[p : p + 1], (rows, lanes)) for p in range(planes)], 0
            )

        part = part - jnp.where(where % rows == 0, spread(syl[slot]) * 0.5, 0.0)
        return part + jnp.where(where % rows == rows - 1, spread(syh[slot]) * 0.5, 0.0)

    for i in range(3):
        value = velocity[i]
        around = -6.0 * value
        for low, high in (
            x_ends(value, vl[i], vh[i], rows),
            y_ends(value, yl[6 + i], yh[6 + i], rows),
            z_ends(value),
        ):
            around = around + high + low
        pull = force[i] + halo_part(i) + viscosity * around
        velocity_new[i] = value + time_step * occupied * pull / density
        displacement_grad[i] = -(dgrad[i] + halo_part(3 + i))


def finish_kernel(place, mine, other, g_in, gb_in, g_mid, gb_mid, g_out, gb_out, small, wide):
    count, height, _ = mine.shape
    part = height - SMALL
    total = jnp.sum(jnp.square(mine[...])) + jnp.sum(jnp.square(other[...]))
    scale = lax.rsqrt(jnp.full((1, 1), total, f32) / NPARAM + norm_eps)
    half, index = place[0], place[1]
    for m in range(count):
        for ref, side in ((mine, half), (other, 1 - half)):
            chunk = side * count + (index ^ m)
            g_mid[pl.ds(pl.multiple_of(chunk * part, part), part), :] = ref[m, :part] * scale
            small[pl.ds(pl.multiple_of(chunk * SMALL, SMALL), SMALL), :] = ref[m, part:] * scale
    wide[...] = jnp.zeros_like(wide)
    wide[:16] = small[:16]
    g_in[...] = wide[...].T[:, :FEAT]
    gb_in[...] = small[10:11]
    g_out[...] = small[16 : 16 + OUT]
    gb_mid[...] = small[32:34]
    gb_out[...] = small[34:35, :OUT]


def shapes(*items):
    return [jax.ShapeDtypeStruct(item, f32) for item in items]


def along(axis, step):
    count = lax.axis_size(axis)
    return [(i, i + step) for i in range(count) if 0 <= i + step < count]


def swap(value, axis, mask):
    return lax.ppermute(value, axis, [(i, i ^ mask) for i in range(lax.axis_size(axis))])


def body(
    material,
    phase,
    clock,
    displacement,
    velocity,
    cotangent,
    material_table,
    w_in,
    b_in,
    w_mid,
    b_mid,
    w_out,
    b_out,
):
    planes, rows, lanes = material.shape
    size = planes * rows
    voxels = size * lanes
    nx, ny = lax.axis_size("gx"), lax.axis_size("gy")
    chunks = 2 * nx
    part = 2 * HID // chunks
    assert chunks >= GROUPS and ny % 2 == 0 and part % 8 == 0
    material = material.reshape(size, lanes)
    phase = phase.reshape(size, lanes)
    displacement = displacement.reshape(3, size, lanes)
    velocity = velocity.reshape(3, size, lanes)
    cotangent = cotangent.reshape(3, size, lanes)

    faces = pl.pallas_call(
        functools.partial(faces_kernel, rows),
        out_shape=shapes(
            *[(6, rows, lanes)] * 2, *[(9, planes, lanes)] * 2, *[(3, rows, lanes)] * 2
        ),
        in_specs=[SMEM] + [VMEM] * 4,
        out_specs=[VMEM] * 6,
        name="faces",
    )(material_table, material, displacement, velocity, cotangent)
    xl = lax.ppermute(faces[0], "gx", along("gx", 1))
    xh = lax.ppermute(faces[1], "gx", along("gx", -1))
    yl = lax.ppermute(faces[2], "gy", along("gy", 1))
    yh = lax.ppermute(faces[3], "gy", along("gy", -1))
    vl = lax.ppermute(faces[4], "gx", along("gx", 1))
    vh = lax.ppermute(faces[5], "gx", along("gx", -1))

    block = 4096
    while voxels % block:
        block //= 2
    outs = pl.pallas_call(
        functools.partial(network_kernel, rows, block),
        out_shape=shapes(
            *[(6, rows, lanes)] * 2,
            *[(6, planes, lanes)] * 2,
            *[(3, size, lanes)] * 2,
            (chunks, part + SMALL, HID),
        ),
        in_specs=[SMEM] * 3 + [VMEM] * 13,
        out_specs=[VMEM] * 7,
        scratch_shapes=[
            pltpu.VMEM((lanes // 128, 16 * size, 128), f32),
            pltpu.VMEM((lanes // 128, 16 * size, 128), f32),
            pltpu.VMEM((16, voxels), bf16),
            pltpu.VMEM((16, voxels), bf16),
            pltpu.VMEM((16, voxels), f32),
            pltpu.VMEM((16, voxels), f32),
            pltpu.VMEM((HID, 16), bf16),
            pltpu.VMEM((16, HID), bf16),
            pltpu.VMEM((2, HID, HID), bf16),
            pltpu.VMEM((16, HID), bf16),
            pltpu.VMEM((HID, 16), bf16),
            pltpu.VMEM((3, HID, 128), f32),
            pltpu.VMEM((2 * HID, HID), f32),
            pltpu.VMEM((16, HID), f32),
            pltpu.VMEM((16, HID), f32),
            pltpu.VMEM((2, HID, 128), f32),
            pltpu.VMEM((16, 128), f32),
            pltpu.VMEM((HID, 128), f32),
            pltpu.VMEM((128, HID), f32),
        ],
        compiler_params=pltpu.CompilerParams(vmem_limit_bytes=50 << 20),
        cost_estimate=pl.CostEstimate(
            flops=6 * voxels * (HID * FEAT + 2 * HID * HID + OUT * HID),
            bytes_accessed=64 * voxels,
            transcendentals=3 * HID * voxels,
        ),
        name="network",
    )(
        material_table,
        clock,
        b_out,
        material,
        phase,
        displacement,
        cotangent,
        xl,
        xh,
        yl,
        yh,
        w_in,
        b_in.reshape(1, HID),
        w_mid,
        b_mid,
        w_out,
    )
    sxl = lax.ppermute(outs[0], "gx", along("gx", 1))
    sxh = lax.ppermute(outs[1], "gx", along("gx", -1))
    syl = lax.ppermute(outs[2], "gy", along("gy", 1))
    syh = lax.ppermute(outs[3], "gy", along("gy", -1))

    half = lax.axis_index("gy") % 2
    index = lax.axis_index("gx")
    pile = outs[6].reshape(2, nx, part + SMALL, HID)
    kept = lax.dynamic_index_in_dim(pile, half, 0, keepdims=False)
    sent = lax.dynamic_index_in_dim(pile, 1 - half, 0, keepdims=False)
    kept = kept + swap(sent, "gy", 1)
    share = lax.dynamic_index_in_dim(kept, index, 0, keepdims=False)
    for m in range(1, nx):
        piece = lax.dynamic_index_in_dim(kept, index ^ m, 0, keepdims=False)
        share = share + swap(piece, "gx", m)
    mask = 2
    while mask < ny:
        share = share + swap(share, "gy", mask)
        mask *= 2
    mine = jnp.stack([share] + [swap(share, "gx", m) for m in range(1, nx)])
    other = swap(mine, "gy", 1)

    fields = pl.pallas_call(
        functools.partial(fields_kernel, rows),
        out_shape=shapes(*[(3, size, lanes)] * 2),
        in_specs=[SMEM] + [VMEM] * 12,
        out_specs=[VMEM] * 2,
        name="fields",
    )(
        material_table,
        material,
        velocity,
        outs[4],
        outs[5],
        vl,
        vh,
        yl,
        yh,
        sxl,
        sxh,
        syl,
        syh,
    )
    place = jnp.stack([half, index]).astype(jnp.int32)
    done = pl.pallas_call(
        finish_kernel,
        out_shape=shapes((HID, FEAT), (1, HID), (2 * HID, HID), (2, HID), (OUT, HID), (1, OUT)),
        in_specs=[SMEM] + [VMEM] * 2,
        out_specs=[VMEM] * 6,
        scratch_shapes=[
            pltpu.VMEM((chunks * SMALL, HID), f32),
            pltpu.VMEM((128, HID), f32),
        ],
        name="finish",
    )(place, mine, other)
    shape = (3, planes, rows, lanes)
    return (
        fields[0].reshape(shape),
        fields[1].reshape(shape),
        done[0],
        done[1].reshape(HID),
        done[2].reshape(2, HID, HID),
        done[3],
        done[4],
        done[5].reshape(OUT),
    )


def solution(mesh):
    in_specs = (
        P("gx", "gy", None),
        P("gx", "gy", None),
        P(),
        P(None, "gx", "gy", None),
        P(None, "gx", "gy", None),
        P(None, "gx", "gy", None),
        P(),
        P(),
        P(),
        P(),
        P(),
        P(),
        P(),
    )
    out_specs = (P(None, "gx", "gy", None), P(None, "gx", "gy", None), P(), P(), P(), P(), P(), P())
    return jax.shard_map(body, mesh=mesh, in_specs=in_specs, out_specs=out_specs, check_vma=False)
```

```python
import functools
import jax
import jax.numpy as jnp
from jax import lax
from jax.experimental import pallas as pl
from jax.experimental.pallas import tpu as pltpu
from jax.sharding import PartitionSpec as P

FEAT = 10
OUT = 9
HID = 256
PHASES = 8
NPARAM = 136713
SMALL = 8
GROUPS = 5

time_step = 0.25
viscosity = 0.2
norm_eps = 1e-06
two_pi = 6.283185307179586

bf16 = jnp.bfloat16
f32 = jnp.float32
VMEM = pl.BlockSpec(memory_space=pltpu.VMEM)
SMEM = pl.BlockSpec(memory_space=pltpu.SMEM)
HBM = pl.BlockSpec(memory_space=pltpu.HBM)


def fetch(sources, targets, sems):
    copies = [
        pltpu.make_async_copy(source, target, sems.at[k])
        for k, (source, target) in enumerate(zip(sources, targets))
    ]
    for copy in copies:
        copy.start()
    return copies


def pick(table, row, material):
    value = jnp.full(material.shape, table[row, 0], f32)
    for kind in range(1, table.shape[1]):
        value = jnp.where(material == kind, table[row, kind], value)
    return value


def step_factor(table, material):
    occupied = jnp.where(material > 0, 1.0, 0.0).astype(f32)
    return occupied, pick(table, 1, material)


def x_ends(field, low, high, rows):
    return (
        jnp.concatenate([low, field[:-rows]], 0),
        jnp.concatenate([field[rows:], high], 0),
    )


def y_ends(field, low, high, rows):
    planes = field.shape[0] // rows
    where = lax.broadcasted_iota(jnp.int32, field.shape, 0)

    def spread(edge):
        return jnp.concatenate(
            [jnp.broadcast_to(edge[p : p + 1], (rows, field.shape[1])) for p in range(planes)], 0
        )

    before, after = pltpu.roll(field, 1, 0), pltpu.roll(field, field.shape[0] - 1, 0)
    low = 0.0 if low is None else spread(low)
    high = 0.0 if high is None else spread(high)
    return (
        jnp.where(where % rows == 0, low, before),
        jnp.where(where % rows == rows - 1, high, after),
    )


def z_ends(field):
    lanes = field.shape[1]
    where = lax.broadcasted_iota(jnp.int32, field.shape, 1)
    return (
        jnp.where(where == 0, 0.0, pltpu.roll(field, 1, 1)),
        jnp.where(where == lanes - 1, 0.0, pltpu.roll(field, lanes - 1, 1)),
    )


def half_diff(ends):
    return (ends[1] - ends[0]) * 0.5


def faces_kernel(rows, *refs):
    sources, (xf, xb, yf, yb), targets, sems = refs[:5], refs[5:9], refs[9:14], refs[14]
    for copy in fetch(sources, targets, sems):
        copy.wait()
    table, material, displacement, velocity, cotangent = targets
    size = material.shape[0]
    planes = size // rows
    occupied, density = step_factor(table, material[...])
    for i in range(3):
        carried = time_step * occupied * cotangent[i] / density
        for slot, field in ((i, displacement[i]), (3 + i, carried), (6 + i, velocity[i])):
            if slot < 6:
                xf[slot] = field[size - rows :]
                xb[slot] = field[:rows]
            for p in range(planes):
                yf[slot, p : p + 1] = field[(p + 1) * rows - 1 : (p + 1) * rows]
                yb[slot, p : p + 1] = field[p * rows : p * rows + 1]


def network_kernel(rows, block, *refs):
    sources, refs = refs[:13], refs[13:]
    (xl, xh, yl, yh), refs = refs[:4], refs[4:]
    (sxf, sxb, syf, syb, force, dgrad, grads), refs = refs[:7], refs[7:]
    targets, sems, refs = refs[:13], refs[13], refs[14:]
    grid_in, grid_delta, feats, delta, net, back, refs = *refs[:6], refs[6:]
    win, winT, wmidT, wout, woutT, bias, refs = *refs[:6], refs[6:]
    acc_mid, acc_in, acc_out, acc_b, acc_bo, wide = refs
    copies = fetch(sources, targets, sems)
    for ref in (acc_mid, acc_in, acc_out, acc_b, acc_bo):
        ref[...] = jnp.zeros_like(ref)
    for copy in copies:
        copy.wait()
    table, clock, b_out, material, phase, displacement, cotangent, velocity = targets[:8]
    w_inT, b_in, w_mid, b_mid, w_out = targets[8:]
    size, lanes = material.shape
    planes = size // rows
    tiles = lanes // 128
    voxels = size * lanes
    mat = material[...]
    occupied, density = step_factor(table, mat)
    strength = occupied * pick(table, 0, mat)

    wide[...] = jnp.zeros_like(wide)
    wide[:FEAT] = w_inT[...].astype(f32)
    winT[...] = wide[:16].astype(bf16)
    win[...] = wide[...].T[:, :16].astype(bf16)
    wide[...] = jnp.zeros_like(wide)
    wide[:OUT] = w_out[...].astype(f32)
    wout[...] = wide[:16].astype(bf16)
    woutT[...] = wide[...].T[:, :16].astype(bf16)
    for k in range(2):
        wmidT[k] = w_mid[k].astype(f32).T.astype(bf16)
    for k, row in enumerate((b_in[...], b_mid[0:1], b_mid[1:2])):
        bias[k] = jnp.broadcast_to(row, (128, HID)).T

    def put(ref, slot, field):
        for t in range(tiles):
            ref[t, slot * size : (slot + 1) * size] = field[:, t * 128 : (t + 1) * 128]

    factor = time_step * occupied
    for i in range(3):
        field = displacement[i]
        put(grid_in, 3 * i, half_diff(x_ends(field, xl[i], xh[i], rows)))
        put(grid_in, 3 * i + 1, half_diff(y_ends(field, yl[i], yh[i], rows)))
        put(grid_in, 3 * i + 2, half_diff(z_ends(field)))
        field = factor * cotangent[i] / density
        put(grid_delta, 3 * i, strength * -half_diff(x_ends(field, xl[3 + i], xh[3 + i], rows)))
        put(grid_delta, 3 * i + 1, strength * -half_diff(y_ends(field, yl[3 + i], yh[3 + i], rows)))
        put(grid_delta, 3 * i + 2, strength * -half_diff(z_ends(field)))
    put(grid_in, 9, jnp.sin(two_pi * phase[...].astype(f32) / PHASES + clock[0]))
    put(grid_in, 10, jnp.ones((size, lanes), f32))
    for slot in range(11, 16):
        put(grid_in, slot, jnp.zeros((size, lanes), f32))
    for slot in range(9, 16):
        put(grid_delta, slot, jnp.zeros((size, lanes), f32))
    for r in range(size):
        for t in range(tiles):
            at = slice((r * tiles + t) * 128, (r * tiles + t + 1) * 128)
            feats[:, at] = grid_in[t, pl.ds(r, 16, stride=size), :].astype(bf16)
            delta[:, at] = grid_delta[t, pl.ds(r, 16, stride=size), :].astype(bf16)

    rowid = lax.broadcasted_iota(jnp.int32, (16, 1), 0)
    bias_out = jnp.zeros((16, 1), f32)
    for k in range(OUT):
        bias_out = jnp.where(rowid == k, b_out[k], bias_out)

    def mul(a, b):
        return jnp.dot(a, b, preferred_element_type=f32)

    def mul_t(a, b):
        return lax.dot_general(a, b, (((1,), (1,)), ((), ())), preferred_element_type=f32)

    def lane_sum(value):
        total = value[:, :128].astype(f32)
        for k in range(1, block // 128):
            total = total + value[:, k * 128 : (k + 1) * 128].astype(f32)
        return total

    def slope(value):
        wider = value.astype(f32)
        return 1.0 - wider * wider

    def step(index, carry):
        at = pl.ds(pl.multiple_of(index * block, block), block)
        f, d = feats[:, at], delta[:, at]
        h1 = jnp.tanh(mul(win[...], f) + bias[0][:, :1]).astype(bf16)
        h2 = jnp.tanh(mul(w_mid[0], h1) + bias[1][:, :1]).astype(bf16)
        h3 = jnp.tanh(mul(w_mid[1], h2) + bias[2][:, :1]).astype(bf16)
        net[:, at] = mul(wout[...], h3) + bias_out
        acc_out[...] += mul_t(d, h3)
        acc_bo[...] += lane_sum(d)
        d3 = (mul(woutT[...], d) * slope(h3)).astype(bf16)
        acc_mid[HID:] += mul_t(d3, h2)
        acc_b[1] += lane_sum(d3)
        d2 = (mul(wmidT[1], d3) * slope(h2)).astype(bf16)
        acc_mid[:HID] += mul_t(d2, h1)
        acc_b[0] += lane_sum(d2)
        d1 = (mul(wmidT[0], d2) * slope(h1)).astype(bf16)
        acc_in[...] += mul_t(f, d1)
        back[:, at] = mul(winT[...], d1)
        return carry

    lax.fori_loop(0, voxels // block, step, 0)

    for r in range(size):
        for t in range(tiles):
            at = slice((r * tiles + t) * 128, (r * tiles + t + 1) * 128)
            grid_in[t, pl.ds(r, 16, stride=size), :] = net[:, at]
            grid_delta[t, pl.ds(r, 16, stride=size), :] = back[:, at]

    def get(ref, slot):
        return jnp.concatenate(
            [ref[t, slot * size : (slot + 1) * size] for t in range(tiles)], axis=1
        )

    for i in range(3):
        sxf[6 + i] = velocity[i, size - rows :]
        sxb[6 + i] = velocity[i, :rows]
    nothing = jnp.zeros((rows, lanes), f32)
    for base, ref, scale, out in ((0, grid_in, strength, force), (3, grid_delta, None, dgrad)):
        for i in range(3):
            along = [get(ref, 3 * i + j) for j in range(3)]
            if scale is not None:
                along = [scale * item for item in along]
            slot = base + i
            sxf[slot] = along[0][size - rows :]
            sxb[slot] = along[0][:rows]
            for p in range(planes):
                syf[slot, p : p + 1] = along[1][(p + 1) * rows - 1 : (p + 1) * rows]
                syb[slot, p : p + 1] = along[1][p * rows : p * rows + 1]
            out[i] = (
                half_diff(x_ends(along[0], nothing, nothing, rows))
                + half_diff(y_ends(along[1], None, None, rows))
                + half_diff(z_ends(along[2]))
            )

    chunks = grads.shape[0]
    part = 2 * HID // chunks
    for c in range(chunks):
        grads[c, :part] = acc_mid[c * part : (c + 1) * part]
        grads[c, part:] = jnp.zeros((SMALL, HID), f32)
    grads[0, part:] = acc_in[:8]
    grads[1, part:] = jnp.where(rowid[:8] < 3, acc_in[8:], 0.0)
    grads[2, part:] = acc_out[:8]
    grads[3, part:] = acc_out[8:]
    for k in range(2):
        grads[4, part + k : part + k + 1] = jnp.sum(acc_b[k].T, axis=0, keepdims=True)
    wide[...] = jnp.zeros_like(wide)
    wide[:16, :128] = acc_bo[...]
    grads[4, part + 2 : part + 3, :128] = jnp.sum(wide[:, :128].T, axis=0, keepdims=True)


def fields_kernel(
    rows,
    table,
    material,
    velocity,
    force,
    dgrad,
    yl,
    yh,
    sxl,
    sxh,
    syl,
    syh,
    velocity_new,
    displacement_grad,
):
    size, lanes = material.shape
    planes = size // rows
    occupied, density = step_factor(table, material[...])

    def halo_part(slot):
        middle = [jnp.zeros((rows, lanes), f32)] * (planes - 2)
        first, last = -0.5 * sxl[slot], 0.5 * sxh[slot]
        part = jnp.concatenate([first, *middle, last] if planes > 1 else [first + last], 0)
        where = lax.broadcasted_iota(jnp.int32, (size, lanes), 0)

        def spread(edge):
            return jnp.concatenate(
                [jnp.broadcast_to(edge[p : p + 1], (rows, lanes)) for p in range(planes)], 0
            )

        part = part - jnp.where(where % rows == 0, spread(syl[slot]) * 0.5, 0.0)
        return part + jnp.where(where % rows == rows - 1, spread(syh[slot]) * 0.5, 0.0)

    for i in range(3):
        value = velocity[i]
        around = -6.0 * value
        for low, high in (
            x_ends(value, sxl[6 + i], sxh[6 + i], rows),
            y_ends(value, yl[6 + i], yh[6 + i], rows),
            z_ends(value),
        ):
            around = around + high + low
        pull = force[i] + halo_part(i) + viscosity * around
        velocity_new[i] = value + time_step * occupied * pull / density
        displacement_grad[i] = -(dgrad[i] + halo_part(3 + i))


def finish_kernel(place, mine, other, g_in, gb_in, g_mid, gb_mid, g_out, gb_out, small):
    count, height, _ = mine.shape
    part = height - SMALL
    total = jnp.sum(jnp.square(mine[...])) + jnp.sum(jnp.square(other[...]))
    scale = lax.rsqrt(jnp.full((1, 1), total, f32) / NPARAM + norm_eps)
    half, index = place[0], place[1]
    for m in range(count):
        for ref, side in ((mine, half), (other, 1 - half)):
            chunk = side * count + (index ^ m)
            g_mid[pl.ds(pl.multiple_of(chunk * part, part), part), :] = ref[m, :part] * scale
            small[pl.ds(pl.multiple_of(chunk * SMALL, SMALL), SMALL), :] = ref[m, part:] * scale
    g_in[...] = small[:FEAT]
    gb_in[...] = small[10:11]
    g_out[...] = small[16 : 16 + OUT]
    gb_mid[...] = small[32:34]
    gb_out[...] = small[34:35, :OUT]


def shapes(*items):
    return [jax.ShapeDtypeStruct(item, f32) for item in items]


def stay(value):
    if value.size < 2:
        return value
    return pltpu.with_memory_space_constraint(value, pltpu.HBM)


def along(axis, step):
    count = lax.axis_size(axis)
    return [(i, i + step) for i in range(count) if 0 <= i + step < count]


def swap(value, axis, mask):
    return lax.ppermute(value, axis, [(i, i ^ mask) for i in range(lax.axis_size(axis))])


def body(
    material,
    phase,
    clock,
    displacement,
    velocity,
    cotangent,
    material_table,
    w_in,
    b_in,
    w_mid,
    b_mid,
    w_out,
    b_out,
):
    planes, rows, lanes = material.shape
    size = planes * rows
    voxels = size * lanes
    nx, ny = lax.axis_size("gx"), lax.axis_size("gy")
    chunks = 2 * nx
    part = 2 * HID // chunks
    assert chunks >= GROUPS and ny % 2 == 0 and part % 8 == 0
    material = material.reshape(size, lanes)
    phase = phase.reshape(size, lanes)
    displacement = displacement.reshape(3, size, lanes)
    velocity = velocity.reshape(3, size, lanes)
    cotangent = cotangent.reshape(3, size, lanes)

    faces = pl.pallas_call(
        functools.partial(faces_kernel, rows),
        out_shape=shapes(
            *[(6, rows, lanes)] * 2, *[(9, planes, lanes)] * 2
        ),
        in_specs=[HBM] * 5,
        out_specs=[VMEM] * 4,
        scratch_shapes=[
            pltpu.SMEM(material_table.shape, f32),
            pltpu.VMEM((size, lanes), jnp.int32),
            *[pltpu.VMEM((3, size, lanes), f32)] * 3,
            pltpu.SemaphoreType.DMA((5,)),
        ],
        compiler_params=pltpu.CompilerParams(vmem_limit_bytes=6 << 20),
        name="faces",
    )(*map(stay, (material_table, material, displacement, velocity, cotangent)))
    xl = lax.ppermute(faces[0], "gx", along("gx", 1))
    xh = lax.ppermute(faces[1], "gx", along("gx", -1))
    yl = lax.ppermute(faces[2], "gy", along("gy", 1))
    yh = lax.ppermute(faces[3], "gy", along("gy", -1))

    block = 4096
    while voxels % block:
        block //= 2
    outs = pl.pallas_call(
        functools.partial(network_kernel, rows, block),
        out_shape=shapes(
            *[(9, rows, lanes)] * 2,
            *[(6, planes, lanes)] * 2,
            *[(3, size, lanes)] * 2,
            (chunks, part + SMALL, HID),
        ),
        in_specs=[HBM] * 13 + [VMEM] * 4,
        out_specs=[VMEM] * 7,
        scratch_shapes=[
            *[pltpu.SMEM(item.shape, f32) for item in (material_table, clock, b_out)],
            *[pltpu.VMEM((size, lanes), jnp.int32)] * 2,
            *[pltpu.VMEM((3, size, lanes), f32)] * 3,
            pltpu.VMEM((FEAT, HID), bf16),
            pltpu.VMEM((1, HID), f32),
            pltpu.VMEM((2, HID, HID), bf16),
            pltpu.VMEM((2, HID), f32),
            pltpu.VMEM((OUT, HID), bf16),
            pltpu.SemaphoreType.DMA((13,)),
            pltpu.VMEM((lanes // 128, 16 * size, 128), f32),
            pltpu.VMEM((lanes // 128, 16 * size, 128), f32),
            pltpu.VMEM((16, voxels), bf16),
            pltpu.VMEM((16, voxels), bf16),
            pltpu.VMEM((16, voxels), f32),
            pltpu.VMEM((16, voxels), f32),
            pltpu.VMEM((HID, 16), bf16),
            pltpu.VMEM((16, HID), bf16),
            pltpu.VMEM((2, HID, HID), bf16),
            pltpu.VMEM((16, HID), bf16),
            pltpu.VMEM((HID, 16), bf16),
            pltpu.VMEM((3, HID, 128), f32),
            pltpu.VMEM((2 * HID, HID), f32),
            pltpu.VMEM((16, HID), f32),
            pltpu.VMEM((16, HID), f32),
            pltpu.VMEM((2, HID, 128), f32),
            pltpu.VMEM((16, 128), f32),
            pltpu.VMEM((128, HID), f32),
        ],
        compiler_params=pltpu.CompilerParams(vmem_limit_bytes=36 << 20),
        cost_estimate=pl.CostEstimate(
            flops=6 * voxels * (HID * FEAT + 2 * HID * HID + OUT * HID),
            bytes_accessed=64 * voxels,
            transcendentals=3 * HID * voxels,
        ),
        name="network",
    )(
        *map(
            stay,
            (
                material_table,
                clock,
                b_out,
                material,
                phase,
                displacement,
                cotangent,
                velocity,
                w_in.T,
                b_in.reshape(1, HID),
                w_mid,
                b_mid,
                w_out,
            ),
        ),
        xl,
        xh,
        yl,
        yh,
    )
    sxl = lax.ppermute(outs[0], "gx", along("gx", 1))
    sxh = lax.ppermute(outs[1], "gx", along("gx", -1))
    syl = lax.ppermute(outs[2], "gy", along("gy", 1))
    syh = lax.ppermute(outs[3], "gy", along("gy", -1))

    half = lax.axis_index("gy") % 2
    index = lax.axis_index("gx")
    pile = outs[6].reshape(2, nx, part + SMALL, HID)
    kept = lax.dynamic_index_in_dim(pile, half, 0, keepdims=False)
    sent = lax.dynamic_index_in_dim(pile, 1 - half, 0, keepdims=False)
    kept = kept + swap(sent, "gy", 1)
    share = lax.dynamic_index_in_dim(kept, index, 0, keepdims=False)
    for m in range(1, nx):
        piece = lax.dynamic_index_in_dim(kept, index ^ m, 0, keepdims=False)
        share = share + swap(piece, "gx", m)
    mask = 2
    while mask < ny:
        share = share + swap(share, "gy", mask)
        mask *= 2
    share, sxl, sxh, syl, syh = lax.optimization_barrier((share, sxl, sxh, syl, syh))
    mine = jnp.stack([share] + [swap(share, "gx", m) for m in range(1, nx)])
    other = swap(mine, "gy", 1)

    fields = pl.pallas_call(
        functools.partial(fields_kernel, rows),
        out_shape=shapes(*[(3, size, lanes)] * 2),
        in_specs=[SMEM] + [VMEM] * 10,
        out_specs=[VMEM] * 2,
        compiler_params=pltpu.CompilerParams(vmem_limit_bytes=6 << 20),
        name="fields",
    )(
        material_table,
        material,
        velocity,
        outs[4],
        outs[5],
        yl,
        yh,
        sxl,
        sxh,
        syl,
        syh,
    )
    place = jnp.stack([half, index]).astype(jnp.int32)
    done = pl.pallas_call(
        finish_kernel,
        out_shape=shapes((FEAT, HID), (1, HID), (2 * HID, HID), (2, HID), (OUT, HID), (1, OUT)),
        in_specs=[SMEM] + [VMEM] * 2,
        out_specs=[VMEM] * 6,
        scratch_shapes=[pltpu.VMEM((chunks * SMALL, HID), f32)],
        compiler_params=pltpu.CompilerParams(vmem_limit_bytes=6 << 20),
        name="finish",
    )(place, mine, other)
    shape = (3, planes, rows, lanes)
    return (
        fields[0].reshape(shape),
        fields[1].reshape(shape),
        done[0].T,
        done[1].reshape(HID),
        done[2].reshape(2, HID, HID),
        done[3],
        done[4],
        done[5].reshape(OUT),
    )


def solution(mesh):
    in_specs = (
        P("gx", "gy", None),
        P("gx", "gy", None),
        P(),
        P(None, "gx", "gy", None),
        P(None, "gx", "gy", None),
        P(None, "gx", "gy", None),
        P(),
        P(),
        P(),
        P(),
        P(),
        P(),
        P(),
    )
    out_specs = (P(None, "gx", "gy", None), P(None, "gx", "gy", None), P(), P(), P(), P(), P(), P())
    return jax.shard_map(body, mesh=mesh, in_specs=in_specs, out_specs=out_specs, check_vma=False)
```

```python
import functools
import jax
import jax.numpy as jnp
from jax import lax
from jax.experimental import pallas as pl
from jax.experimental.pallas import tpu as pltpu
from jax.sharding import PartitionSpec as P

FEAT = 10
OUT = 9
HID = 256
PHASES = 8
NPARAM = 136713
SMALL = 8
GROUPS = 5

time_step = 0.25
viscosity = 0.2
norm_eps = 1e-06
two_pi = 6.283185307179586

bf16 = jnp.bfloat16
f32 = jnp.float32
VMEM = pl.BlockSpec(memory_space=pltpu.VMEM)
SMEM = pl.BlockSpec(memory_space=pltpu.SMEM)
HBM = pl.BlockSpec(memory_space=pltpu.HBM)


def fetch(sources, targets, sems):
    copies = [
        pltpu.make_async_copy(source, target, sems.at[k])
        for k, (source, target) in enumerate(zip(sources, targets))
    ]
    for copy in copies:
        copy.start()
    return copies


def pick(table, row, material):
    value = jnp.full(material.shape, table[row, 0], f32)
    for kind in range(1, table.shape[1]):
        value = jnp.where(material == kind, table[row, kind], value)
    return value


def step_factor(table, material):
    occupied = jnp.where(material > 0, 1.0, 0.0).astype(f32)
    return occupied, pick(table, 1, material)


def x_ends(field, low, high, rows):
    return (
        jnp.concatenate([low, field[:-rows]], 0),
        jnp.concatenate([field[rows:], high], 0),
    )


def y_ends(field, low, high, rows):
    planes = field.shape[0] // rows
    where = lax.broadcasted_iota(jnp.int32, field.shape, 0)

    def spread(edge):
        return jnp.concatenate(
            [jnp.broadcast_to(edge[p : p + 1], (rows, field.shape[1])) for p in range(planes)], 0
        )

    before, after = pltpu.roll(field, 1, 0), pltpu.roll(field, field.shape[0] - 1, 0)
    low = 0.0 if low is None else spread(low)
    high = 0.0 if high is None else spread(high)
    return (
        jnp.where(where % rows == 0, low, before),
        jnp.where(where % rows == rows - 1, high, after),
    )


def z_ends(field):
    lanes = field.shape[1]
    where = lax.broadcasted_iota(jnp.int32, field.shape, 1)
    return (
        jnp.where(where == 0, 0.0, pltpu.roll(field, 1, 1)),
        jnp.where(where == lanes - 1, 0.0, pltpu.roll(field, lanes - 1, 1)),
    )


def half_diff(ends):
    return (ends[1] - ends[0]) * 0.5


def faces_kernel(rows, *refs):
    sources, (xf, xb, yf, yb), targets, sems = refs[:5], refs[5:9], refs[9:14], refs[14]
    for copy in fetch(sources, targets, sems):
        copy.wait()
    table, material, displacement, velocity, cotangent = targets
    occupied, density = step_factor(table, material[...])
    for i in range(3):
        carried = time_step * occupied * cotangent[i] / density
        for slot, field in ((i, displacement[i]), (3 + i, carried), (6 + i, velocity[i])):
            if slot < 6:
                xf[slot] = field[rows:]
            xb[slot] = field[:rows]
            for p in range(2):
                yf[slot, p : p + 1] = field[(p + 1) * rows - 1 : (p + 1) * rows]
                yb[slot, p : p + 1] = field[p * rows : p * rows + 1]


def network_kernel(plane, rows, block, *refs):
    sources, refs = refs[: 12 - plane * 3], refs[12 - plane * 3 :]
    (edge, yl, yh), refs = refs[:3], refs[3:]
    if plane:
        (yf_first, yb_first), given, refs = refs[:2], refs[2:13], refs[13:]
        (sx, yf, yb, rest, grads), refs = refs[:5], refs[5:]
    else:
        (sx, yf, yb, rest), kept, refs = refs[:4], refs[4:15], refs[15:]
    targets, sems, refs = refs[: len(sources)], refs[len(sources)], refs[len(sources) + 1 :]
    grid_in, grid_delta, feats, delta, net, back, wide, *refs = refs
    copies = fetch(sources, targets, sems)
    if plane:
        acc_mid, acc_in, acc_out, acc_b, acc_bo = refs
        win, winT, wmidT, wout, woutT, bias = given[5:]
        for ref, source in zip(refs, given[:5]):
            ref[...] = source[...]
    else:
        acc_mid, acc_in, acc_out, acc_b, acc_bo = kept[:5]
        win, winT, wmidT, wout, woutT, bias = kept[5:]
        for ref in kept[:5]:
            ref[...] = jnp.zeros_like(ref)
    for copy in copies:
        copy.wait()
    table, clock, b_out, material, phase, displacement, cotangent, w_mid = targets[:8]
    lanes = material.shape[1]
    tiles = lanes // 128
    voxels = rows * lanes
    own = slice(plane * rows, (plane + 1) * rows)
    occupied, density = step_factor(table, material[...])
    strength = (occupied * pick(table, 0, material[...]))[own]

    if not plane:
        w_inT, b_in, b_mid, w_out = targets[8:]
        wide[...] = jnp.zeros_like(wide)
        wide[:FEAT] = w_inT[...].astype(f32)
        winT[...] = wide[:16].astype(bf16)
        win[...] = wide[...].T[:, :16].astype(bf16)
        wide[...] = jnp.zeros_like(wide)
        wide[:OUT] = w_out[...].astype(f32)
        wout[...] = wide[:16].astype(bf16)
        woutT[...] = wide[...].T[:, :16].astype(bf16)
        for k in range(2):
            wmidT[k] = w_mid[k].astype(f32).T.astype(bf16)
        for k, row in enumerate((b_in[...], b_mid[0:1], b_mid[1:2])):
            bias[k] = jnp.broadcast_to(row, (128, HID)).T

    def put(ref, slot, field):
        for t in range(tiles):
            ref[t, slot * rows : (slot + 1) * rows] = field[:, t * 128 : (t + 1) * 128]

    def strains(field, slot):
        mine = field[own]
        ends = (field[:rows], edge[slot]) if plane else (edge[slot], field[rows:])
        low, high = yl[slot, plane : plane + 1], yh[slot, plane : plane + 1]
        return half_diff(ends), half_diff(y_ends(mine, low, high, rows)), half_diff(z_ends(mine))

    factor = time_step * occupied
    for i in range(3):
        for j, value in enumerate(strains(displacement[i], i)):
            put(grid_in, 3 * i + j, value)
        for j, value in enumerate(strains(factor * cotangent[i] / density, 3 + i)):
            put(grid_delta, 3 * i + j, strength * -value)
    put(grid_in, 9, jnp.sin(two_pi * phase[own].astype(f32) / PHASES + clock[0]))
    put(grid_in, 10, jnp.ones((rows, lanes), f32))
    for slot in range(11, 16):
        put(grid_in, slot, jnp.zeros((rows, lanes), f32))
    for slot in range(9, 16):
        put(grid_delta, slot, jnp.zeros((rows, lanes), f32))
    for r in range(rows):
        for t in range(tiles):
            at = slice((r * tiles + t) * 128, (r * tiles + t + 1) * 128)
            feats[:, at] = grid_in[t, pl.ds(r, 16, stride=rows), :].astype(bf16)
            delta[:, at] = grid_delta[t, pl.ds(r, 16, stride=rows), :].astype(bf16)

    rowid = lax.broadcasted_iota(jnp.int32, (16, 1), 0)
    bias_out = jnp.zeros((16, 1), f32)
    for k in range(OUT):
        bias_out = jnp.where(rowid == k, b_out[k], bias_out)

    def mul(a, b):
        return jnp.dot(a, b, preferred_element_type=f32)

    def mul_t(a, b):
        return lax.dot_general(a, b, (((1,), (1,)), ((), ())), preferred_element_type=f32)

    def lane_sum(value):
        total = value[:, :128].astype(f32)
        for k in range(1, block // 128):
            total = total + value[:, k * 128 : (k + 1) * 128].astype(f32)
        return total

    def slope(value):
        wider = value.astype(f32)
        return 1.0 - wider * wider

    def step(index, carry):
        at = pl.ds(pl.multiple_of(index * block, block), block)
        f, d = feats[:, at], delta[:, at]
        h1 = jnp.tanh(mul(win[...], f) + bias[0][:, :1]).astype(bf16)
        h2 = jnp.tanh(mul(w_mid[0], h1) + bias[1][:, :1]).astype(bf16)
        h3 = jnp.tanh(mul(w_mid[1], h2) + bias[2][:, :1]).astype(bf16)
        net[:, at] = mul(wout[...], h3) + bias_out
        acc_out[...] += mul_t(d, h3)
        acc_bo[...] += lane_sum(d)
        d3 = (mul(woutT[...], d) * slope(h3)).astype(bf16)
        acc_mid[HID:] += mul_t(d3, h2)
        acc_b[1] += lane_sum(d3)
        d2 = (mul(wmidT[1], d3) * slope(h2)).astype(bf16)
        acc_mid[:HID] += mul_t(d2, h1)
        acc_b[0] += lane_sum(d2)
        d1 = (mul(wmidT[0], d2) * slope(h1)).astype(bf16)
        acc_in[...] += mul_t(f, d1)
        back[:, at] = mul(winT[...], d1)
        return carry

    lax.fori_loop(0, voxels // block, step, 0)

    for r in range(rows):
        for t in range(tiles):
            at = slice((r * tiles + t) * 128, (r * tiles + t + 1) * 128)
            grid_in[t, pl.ds(r, 16, stride=rows), :] = net[:, at]
            grid_delta[t, pl.ds(r, 16, stride=rows), :] = back[:, at]

    def get(ref, slot):
        return jnp.concatenate(
            [ref[t, slot * rows : (slot + 1) * rows] for t in range(tiles)], axis=1
        )

    for base, ref, scale in ((0, grid_in, strength), (3, grid_delta, None)):
        for i in range(3):
            along = [get(ref, 3 * i + j) for j in range(3)]
            if scale is not None:
                along = [scale * item for item in along]
            slot = base + i
            sx[slot] = along[0]
            yf[slot, plane : plane + 1] = along[1][rows - 1 :]
            yb[slot, plane : plane + 1] = along[1][:1]
            if plane:
                yf[slot, 0:1] = yf_first[slot, 0:1]
                yb[slot, 0:1] = yb_first[slot, 0:1]
            rest[slot] = half_diff(y_ends(along[1], None, None, rows)) + half_diff(
                z_ends(along[2])
            )
    if not plane:
        return
    for i in range(3):
        sx[6 + i] = targets[8][i, own]

    chunks = grads.shape[0]
    part = 2 * HID // chunks
    for c in range(chunks):
        grads[c, :part] = acc_mid[c * part : (c + 1) * part]
        grads[c, part:] = jnp.zeros((SMALL, HID), f32)
    grads[0, part:] = acc_in[:8]
    grads[1, part:] = jnp.where(rowid[:8] < 3, acc_in[8:], 0.0)
    grads[2, part:] = acc_out[:8]
    grads[3, part:] = acc_out[8:]
    for k in range(2):
        grads[4, part + k : part + k + 1] = jnp.sum(acc_b[k].T, axis=0, keepdims=True)
    wide[...] = jnp.zeros_like(wide)
    wide[:16, :128] = acc_bo[...]
    grads[4, part + 2 : part + 3, :128] = jnp.sum(wide[:, :128].T, axis=0, keepdims=True)


def fields_kernel(
    rows,
    table,
    material,
    velocity,
    first,
    second,
    rest_first,
    rest_second,
    xh,
    yl,
    yh,
    sxl,
    sxh,
    syl,
    syh,
    velocity_new,
    displacement_grad,
):
    size, lanes = material.shape
    occupied, density = step_factor(table, material[...])
    where = lax.broadcasted_iota(jnp.int32, (size, lanes), 0)

    def spread(edge):
        return jnp.concatenate(
            [jnp.broadcast_to(edge[p : p + 1], (rows, lanes)) for p in range(2)], 0
        )

    def total(slot):
        value = jnp.concatenate(
            [
                rest_first[slot] + half_diff((sxl[slot], second[slot])),
                rest_second[slot] + half_diff((first[slot], sxh[slot])),
            ],
            0,
        )
        value = value - jnp.where(where % rows == 0, spread(syl[slot]) * 0.5, 0.0)
        return value + jnp.where(where % rows == rows - 1, spread(syh[slot]) * 0.5, 0.0)

    for i in range(3):
        value = velocity[i]
        around = -6.0 * value
        for low, high in (
            x_ends(value, sxl[6 + i], xh[6 + i], rows),
            y_ends(value, yl[6 + i], yh[6 + i], rows),
            z_ends(value),
        ):
            around = around + high + low
        pull = total(i) + viscosity * around
        velocity_new[i] = value + time_step * occupied * pull / density
        displacement_grad[i] = -total(3 + i)


def finish_kernel(place, mine, other, g_in, gb_in, g_mid, gb_mid, g_out, gb_out, small):
    count, height, _ = mine.shape
    part = height - SMALL
    total = jnp.sum(jnp.square(mine[...])) + jnp.sum(jnp.square(other[...]))
    scale = lax.rsqrt(jnp.full((1, 1), total, f32) / NPARAM + norm_eps)
    half, index = place[0], place[1]
    for m in range(count):
        for ref, side in ((mine, half), (other, 1 - half)):
            chunk = side * count + (index ^ m)
            g_mid[pl.ds(pl.multiple_of(chunk * part, part), part), :] = ref[m, :part] * scale
            small[pl.ds(pl.multiple_of(chunk * SMALL, SMALL), SMALL), :] = ref[m, part:] * scale
    g_in[...] = small[:FEAT]
    gb_in[...] = small[10:11]
    g_out[...] = small[16 : 16 + OUT]
    gb_mid[...] = small[32:34]
    gb_out[...] = small[34:35, :OUT]


def shapes(*items):
    return [jax.ShapeDtypeStruct(item, f32) for item in items]


def stay(value):
    if value.size < 2:
        return value
    return pltpu.with_memory_space_constraint(value, pltpu.HBM)


def along(axis, step):
    count = lax.axis_size(axis)
    return [(i, i + step) for i in range(count) if 0 <= i + step < count]


def swap(value, axis, mask):
    return lax.ppermute(value, axis, [(i, i ^ mask) for i in range(lax.axis_size(axis))])


def body(
    material,
    phase,
    clock,
    displacement,
    velocity,
    cotangent,
    material_table,
    w_in,
    b_in,
    w_mid,
    b_mid,
    w_out,
    b_out,
):
    planes, rows, lanes = material.shape
    size = planes * rows
    nx, ny = lax.axis_size("gx"), lax.axis_size("gy")
    chunks = 2 * nx
    part = 2 * HID // chunks
    assert planes == 2 and chunks >= GROUPS and ny % 2 == 0 and part % 8 == 0
    material = material.reshape(size, lanes)
    phase = phase.reshape(size, lanes)
    displacement = displacement.reshape(3, size, lanes)
    velocity = velocity.reshape(3, size, lanes)
    cotangent = cotangent.reshape(3, size, lanes)

    faces = pl.pallas_call(
        functools.partial(faces_kernel, rows),
        out_shape=shapes((6, rows, lanes), (9, rows, lanes), *[(9, 2, lanes)] * 2),
        in_specs=[HBM] * 5,
        out_specs=[VMEM] * 4,
        scratch_shapes=[
            pltpu.SMEM(material_table.shape, f32),
            pltpu.VMEM((size, lanes), jnp.int32),
            *[pltpu.VMEM((3, size, lanes), f32)] * 3,
            pltpu.SemaphoreType.DMA((5,)),
        ],
        compiler_params=pltpu.CompilerParams(vmem_limit_bytes=6 << 20),
        name="faces",
    )(*map(stay, (material_table, material, displacement, velocity, cotangent)))
    xl = lax.ppermute(faces[0], "gx", along("gx", 1))
    yl = lax.ppermute(faces[2], "gy", along("gy", 1))
    yh = lax.ppermute(faces[3], "gy", along("gy", -1))
    xh = lax.ppermute(faces[1], "gx", along("gx", -1))

    voxels = rows * lanes
    block = 4096
    while voxels % block:
        block //= 2
    handed = [
        ((2 * HID, HID), f32),
        ((16, HID), f32),
        ((16, HID), f32),
        ((2, HID, 128), f32),
        ((16, 128), f32),
        ((HID, 16), bf16),
        ((16, HID), bf16),
        ((2, HID, HID), bf16),
        ((16, HID), bf16),
        ((HID, 16), bf16),
        ((3, HID, 128), f32),
    ]

    def network(plane, sources, near):
        outs = [jax.ShapeDtypeStruct(*item) for item in handed]
        if plane:
            outs = shapes((chunks, part + SMALL, HID))
        return pl.pallas_call(
            functools.partial(network_kernel, plane, rows, block),
            out_shape=shapes(
                (6 + 3 * plane, rows, lanes), *[(6, 1 + plane, lanes)] * 2, (6, rows, lanes)
            )
            + outs,
            in_specs=[HBM] * len(sources) + [VMEM] * len(near),
            out_specs=[VMEM] * (4 + len(outs)),
            scratch_shapes=[
                *[pltpu.SMEM(item.shape, f32) for item in sources[:3]],
                *[pltpu.VMEM(item.shape, item.dtype) for item in sources[3:]],
                pltpu.SemaphoreType.DMA((len(sources),)),
                *[pltpu.VMEM((lanes // 128, 16 * rows, 128), f32)] * 2,
                *[pltpu.VMEM((16, voxels), bf16)] * 2,
                *[pltpu.VMEM((16, voxels), f32)] * 2,
                pltpu.VMEM((128, HID), f32),
                *[pltpu.VMEM(*item) for item in handed[: 5 * plane]],
            ],
            compiler_params=pltpu.CompilerParams(vmem_limit_bytes=36 << 20),
            cost_estimate=pl.CostEstimate(
                flops=6 * voxels * (HID * FEAT + 2 * HID * HID + OUT * HID),
                bytes_accessed=64 * voxels,
                transcendentals=3 * HID * voxels,
            ),
            name="network",
        )(*map(stay, sources), *near)

    common = [material_table, clock, b_out, material, phase, displacement, cotangent, w_mid]
    first = network(
        0, common + [w_in.T, b_in.reshape(1, HID), b_mid, w_out], [xl, yl, yh]
    )
    sxh = lax.ppermute(first[0], "gx", along("gx", -1))
    second = network(1, common + [velocity], [xh, yl, yh, *first[1:3], *first[4:]])
    sxl = lax.ppermute(second[0], "gx", along("gx", 1))

    half = lax.axis_index("gy") % 2
    index = lax.axis_index("gx")
    pile, sxh = lax.optimization_barrier((second[4], sxh))
    pile = pile.reshape(2, nx, part + SMALL, HID)
    kept = lax.dynamic_index_in_dim(pile, half, 0, keepdims=False)
    sent = lax.dynamic_index_in_dim(pile, 1 - half, 0, keepdims=False)
    kept, face = lax.optimization_barrier((kept + swap(sent, "gy", 1), second[1]))
    syl = lax.ppermute(face, "gy", along("gy", 1))
    share = lax.dynamic_index_in_dim(kept, index, 0, keepdims=False)
    for m in range(1, nx):
        piece = lax.dynamic_index_in_dim(kept, index ^ m, 0, keepdims=False)
        share = share + swap(piece, "gx", m)
    share, face = lax.optimization_barrier((share, second[2]))
    syh = lax.ppermute(face, "gy", along("gy", -1))
    mask = 2
    while mask < ny:
        share = share + swap(share, "gy", mask)
        if mask == 2:
            share, sxl, syl = lax.optimization_barrier((share, sxl, syl))
        mask *= 2
    share, syh = lax.optimization_barrier((share, syh))
    mine = jnp.stack([share] + [swap(share, "gx", m) for m in range(1, nx)])

    fields = pl.pallas_call(
        functools.partial(fields_kernel, rows),
        out_shape=shapes(*[(3, size, lanes)] * 2),
        in_specs=[SMEM] + [VMEM] * 13,
        out_specs=[VMEM] * 2,
        compiler_params=pltpu.CompilerParams(vmem_limit_bytes=6 << 20),
        name="fields",
    )(
        stay(material_table),
        stay(material),
        stay(velocity),
        first[0],
        second[0],
        first[3],
        second[3],
        xh,
        yl,
        yh,
        sxl,
        sxh,
        syl,
        syh,
    )
    mine, *fields = lax.optimization_barrier((mine, *fields))
    other = swap(mine, "gy", 1)
    place = jnp.stack([half, index]).astype(jnp.int32)
    done = pl.pallas_call(
        finish_kernel,
        out_shape=shapes((FEAT, HID), (1, HID), (2 * HID, HID), (2, HID), (OUT, HID), (1, OUT)),
        in_specs=[SMEM] + [VMEM] * 2,
        out_specs=[VMEM] * 6,
        scratch_shapes=[pltpu.VMEM((chunks * SMALL, HID), f32)],
        compiler_params=pltpu.CompilerParams(vmem_limit_bytes=6 << 20),
        name="finish",
    )(place, mine, other)
    shape = (3, planes, rows, lanes)
    return (
        fields[0].reshape(shape),
        fields[1].reshape(shape),
        done[0].T,
        done[1].reshape(HID),
        done[2].reshape(2, HID, HID),
        done[3],
        done[4],
        done[5].reshape(OUT),
    )


def solution(mesh):
    in_specs = (
        P("gx", "gy", None),
        P("gx", "gy", None),
        P(),
        P(None, "gx", "gy", None),
        P(None, "gx", "gy", None),
        P(None, "gx", "gy", None),
        P(),
        P(),
        P(),
        P(),
        P(),
        P(),
        P(),
    )
    out_specs = (P(None, "gx", "gy", None), P(None, "gx", "gy", None), P(), P(), P(), P(), P(), P())
    return jax.shard_map(body, mesh=mesh, in_specs=in_specs, out_specs=out_specs, check_vma=False)
```

```python
import functools
import jax
import jax.numpy as jnp
from jax import lax
from jax.experimental import pallas as pl
from jax.experimental.pallas import tpu as pltpu
from jax.sharding import PartitionSpec as P

FEAT = 10
OUT = 9
HID = 256
PHASES = 8
NPARAM = 136713
SMALL = 8
GROUPS = 5

time_step = 0.25
viscosity = 0.2
norm_eps = 1e-06
two_pi = 6.283185307179586

bf16 = jnp.bfloat16
f32 = jnp.float32
VMEM = pl.BlockSpec(memory_space=pltpu.VMEM)
SMEM = pl.BlockSpec(memory_space=pltpu.SMEM)
HBM = pl.BlockSpec(memory_space=pltpu.HBM)


def fetch(sources, targets, sems):
    copies = [
        pltpu.make_async_copy(source, target, sems.at[k])
        for k, (source, target) in enumerate(zip(sources, targets))
    ]
    for copy in copies:
        copy.start()
    return copies


def pick(table, row, material):
    value = jnp.full(material.shape, table[row, 0], f32)
    for kind in range(1, table.shape[1]):
        value = jnp.where(material == kind, table[row, kind], value)
    return value


def step_factor(table, material):
    occupied = jnp.where(material > 0, 1.0, 0.0).astype(f32)
    return occupied, pick(table, 1, material)


def near_first():
    near = 1 - lax.rem(lax.axis_index("gx"), 2)
    return near, lax.rem(lax.axis_index("gy"), 2)


def y_ends(field, low, high, rows):
    where = lax.broadcasted_iota(jnp.int32, field.shape, 0)
    return (
        jnp.where(where == 0, low, pltpu.roll(field, 1, 0)),
        jnp.where(where == rows - 1, high, pltpu.roll(field, rows - 1, 0)),
    )


def z_ends(field):
    lanes = field.shape[1]
    where = lax.broadcasted_iota(jnp.int32, field.shape, 1)
    return (
        jnp.where(where == 0, 0.0, pltpu.roll(field, 1, 1)),
        jnp.where(where == lanes - 1, 0.0, pltpu.roll(field, lanes - 1, 1)),
    )


def half_diff(ends):
    return (ends[1] - ends[0]) * 0.5


def faces_kernel(rows, *refs):
    sources, outs, targets, sems = refs[:5], refs[5:9], refs[9:14], refs[14]
    copies = fetch(sources, targets, sems)
    near, side = near_first()
    for copy in copies:
        copy.wait()
    x_pair, x_next, y_pair, y_next = outs
    table, material, displacement, velocity, cotangent = targets
    for k, plane in enumerate((near, 1 - near)):
        own = pl.ds(pl.multiple_of(plane * rows, rows), rows)
        occupied, density = step_factor(table, material[own])
        for i in range(3):
            carried = time_step * occupied * cotangent[i, own] / density
            moving = velocity[i, own]
            for slot, field in ((i, displacement[i, own]), (3 + i, carried), (6 + i, moving)):
                if k:
                    x_next[slot] = field
                elif slot < 6:
                    x_pair[slot] = field
                y_pair[slot, k : k + 1] = jnp.where(side == 0, field[rows - 1 :], field[:1])
                y_next[slot, k : k + 1] = jnp.where(side == 0, field[:1], field[rows - 1 :])


def low_high(side, pair, following):
    return jnp.where(side == 0, following, pair), jnp.where(side == 0, pair, following)


def network_kernel(order, rows, block, *refs):
    sources, refs = refs[: 13 - order * 5], refs[13 - order * 5 :]
    (edge, y_pair, y_next), refs = refs[:3], refs[3:]
    if order:
        faces_first, given, refs = refs[:2], refs[2:13], refs[13:]
        (sx, s_pair, s_next, rest, grads), refs = refs[:5], refs[5:]
    else:
        (sx, s_pair, s_next, rest), kept, refs = refs[:4], refs[4:15], refs[15:]
    targets, sems, refs = refs[: len(sources)], refs[len(sources)], refs[len(sources) + 1 :]
    grid_in, grid_delta, feats, delta, net, back, wide, *refs = refs
    copies = fetch(sources, targets, sems)
    near, side = near_first()
    if order:
        acc_mid, acc_in, acc_out, acc_b, acc_bo = refs
        win, winT, wmidT, wout, woutT, bias = given[5:]
        for ref, source in zip(refs, given[:5]):
            ref[...] = source[...]
    else:
        acc_mid, acc_in, acc_out, acc_b, acc_bo = kept[:5]
        win, winT, wmidT, wout, woutT, bias = kept[5:]
        for ref in kept[:5]:
            ref[...] = jnp.zeros_like(ref)
    for copy in copies:
        copy.wait()
    table, clock, b_out, material, phase, displacement, cotangent, w_mid = targets[:8]
    lanes = material.shape[1]
    tiles = lanes // 128
    voxels = rows * lanes
    plane = 1 - near if order else near
    own = pl.ds(pl.multiple_of(plane * rows, rows), rows)
    across = pl.ds(pl.multiple_of((1 - plane) * rows, rows), rows)
    occupied, _ = step_factor(table, material[own])
    strength = occupied * pick(table, 0, material[own])

    if not order:
        w_inT, b_in, b_mid, w_out = targets[8:12]
        wide[...] = jnp.zeros_like(wide)
        wide[:FEAT] = w_inT[...].astype(f32)
        winT[...] = wide[:16].astype(bf16)
        win[...] = wide[...].T[:, :16].astype(bf16)
        wide[...] = jnp.zeros_like(wide)
        wide[:OUT] = w_out[...].astype(f32)
        wout[...] = wide[:16].astype(bf16)
        woutT[...] = wide[...].T[:, :16].astype(bf16)
        for k in range(2):
            wmidT[k] = w_mid[k].astype(f32).T.astype(bf16)
        for k, row in enumerate((b_in[...], b_mid[0:1], b_mid[1:2])):
            bias[k] = jnp.broadcast_to(row, (128, HID)).T

    def put(ref, slot, field):
        for t in range(tiles):
            ref[t, slot * rows : (slot + 1) * rows] = field[:, t * 128 : (t + 1) * 128]

    uphill = jnp.where(plane == 0, 0.5, -0.5)

    def strains(mine, other, slot):
        low, high = low_high(
            side, y_pair[slot, order : order + 1], y_next[slot, order : order + 1]
        )
        return (
            (other - edge[slot]) * uphill,
            half_diff(y_ends(mine, low, high, rows)),
            half_diff(z_ends(mine)),
        )

    def carried(rows_of, slot):
        full, thick = step_factor(table, material[rows_of])
        return time_step * full * cotangent[slot, rows_of] / thick

    for i in range(3):
        for j, value in enumerate(strains(displacement[i, own], displacement[i, across], i)):
            put(grid_in, 3 * i + j, value)
        for j, value in enumerate(strains(carried(own, i), carried(across, i), 3 + i)):
            put(grid_delta, 3 * i + j, strength * -value)
    put(grid_in, 9, jnp.sin(two_pi * phase[own].astype(f32) / PHASES + clock[0]))
    put(grid_in, 10, jnp.ones((rows, lanes), f32))
    for slot in range(11, 16):
        put(grid_in, slot, jnp.zeros((rows, lanes), f32))
    for slot in range(9, 16):
        put(grid_delta, slot, jnp.zeros((rows, lanes), f32))
    for r in range(rows):
        for t in range(tiles):
            at = slice((r * tiles + t) * 128, (r * tiles + t + 1) * 128)
            feats[:, at] = grid_in[t, pl.ds(r, 16, stride=rows), :].astype(bf16)
            delta[:, at] = grid_delta[t, pl.ds(r, 16, stride=rows), :].astype(bf16)

    rowid = lax.broadcasted_iota(jnp.int32, (16, 1), 0)
    bias_out = jnp.zeros((16, 1), f32)
    for k in range(OUT):
        bias_out = jnp.where(rowid == k, b_out[k], bias_out)

    def mul(a, b):
        return jnp.dot(a, b, preferred_element_type=f32)

    def mul_t(a, b):
        return lax.dot_general(a, b, (((1,), (1,)), ((), ())), preferred_element_type=f32)

    def lane_sum(value):
        total = value[:, :128].astype(f32)
        for k in range(1, block // 128):
            total = total + value[:, k * 128 : (k + 1) * 128].astype(f32)
        return total

    def slope(value):
        wider = value.astype(f32)
        return 1.0 - wider * wider

    def step(index, carry):
        at = pl.ds(pl.multiple_of(index * block, block), block)
        f, d = feats[:, at], delta[:, at]
        h1 = jnp.tanh(mul(win[...], f) + bias[0][:, :1]).astype(bf16)
        h2 = jnp.tanh(mul(w_mid[0], h1) + bias[1][:, :1]).astype(bf16)
        h3 = jnp.tanh(mul(w_mid[1], h2) + bias[2][:, :1]).astype(bf16)
        net[:, at] = mul(wout[...], h3) + bias_out
        acc_out[...] += mul_t(d, h3)
        acc_bo[...] += lane_sum(d)
        d3 = (mul(woutT[...], d) * slope(h3)).astype(bf16)
        acc_mid[HID:] += mul_t(d3, h2)
        acc_b[1] += lane_sum(d3)
        d2 = (mul(wmidT[1], d3) * slope(h2)).astype(bf16)
        acc_mid[:HID] += mul_t(d2, h1)
        acc_b[0] += lane_sum(d2)
        d1 = (mul(wmidT[0], d2) * slope(h1)).astype(bf16)
        acc_in[...] += mul_t(f, d1)
        back[:, at] = mul(winT[...], d1)
        return carry

    lax.fori_loop(0, voxels // block, step, 0)

    for r in range(rows):
        for t in range(tiles):
            at = slice((r * tiles + t) * 128, (r * tiles + t + 1) * 128)
            grid_in[t, pl.ds(r, 16, stride=rows), :] = net[:, at]
            grid_delta[t, pl.ds(r, 16, stride=rows), :] = back[:, at]

    def get(ref, slot):
        return jnp.concatenate(
            [ref[t, slot * rows : (slot + 1) * rows] for t in range(tiles)], axis=1
        )

    for base, ref, scale in ((0, grid_in, strength), (3, grid_delta, None)):
        for i in range(3):
            along = [get(ref, 3 * i + j) for j in range(3)]
            if scale is not None:
                along = [scale * item for item in along]
            slot = base + i
            sx[slot] = along[0]
            first, last = along[1][:1], along[1][rows - 1 :]
            s_pair[slot, order : order + 1] = jnp.where(side == 0, last, first)
            s_next[slot, order : order + 1] = jnp.where(side == 0, first, last)
            if order:
                s_pair[slot, 0:1] = faces_first[0][slot, 0:1]
                s_next[slot, 0:1] = faces_first[1][slot, 0:1]
            rest[slot] = half_diff(y_ends(along[1], 0.0, 0.0, rows)) + half_diff(
                z_ends(along[2])
            )
    if not order:
        for i in range(3):
            sx[6 + i] = targets[12][i, own]
        return

    chunks = grads.shape[0]
    part = 2 * HID // chunks
    for c in range(chunks):
        grads[c, :part] = acc_mid[c * part : (c + 1) * part]
        grads[c, part:] = jnp.zeros((SMALL, HID), f32)
    grads[0, part:] = acc_in[:8]
    grads[1, part:] = jnp.where(rowid[:8] < 3, acc_in[8:], 0.0)
    grads[2, part:] = acc_out[:8]
    grads[3, part:] = acc_out[8:]
    for k in range(2):
        grads[4, part + k : part + k + 1] = jnp.sum(acc_b[k].T, axis=0, keepdims=True)
    wide[...] = jnp.zeros_like(wide)
    wide[:16, :128] = acc_bo[...]
    grads[4, part + 2 : part + 3, :128] = jnp.sum(wide[:, :128].T, axis=0, keepdims=True)


def fields_kernel(
    rows,
    table,
    material,
    velocity,
    stress_near,
    stress_far,
    rest_near,
    rest_far,
    x_next,
    y_pair,
    y_next,
    sx_pair,
    sx_next,
    sy_pair,
    sy_next,
    velocity_new,
    displacement_grad,
):
    near, side = near_first()
    lanes = material.shape[1]
    where = lax.broadcasted_iota(jnp.int32, (rows, lanes), 0)
    for k, plane in enumerate((near, 1 - near)):
        own = pl.ds(pl.multiple_of(plane * rows, rows), rows)
        across = pl.ds(pl.multiple_of((1 - plane) * rows, rows), rows)
        occupied, density = step_factor(table, material[own])
        uphill = jnp.where(plane == 0, 0.5, -0.5)
        other, edge = (stress_near, sx_next) if k else (stress_far, sx_pair)
        moving, rest = (x_next, rest_far) if k else (sx_pair, rest_near)

        def total(slot):
            low, high = low_high(side, sy_pair[slot, k : k + 1], sy_next[slot, k : k + 1])
            value = rest[slot] + (other[slot] - edge[slot]) * uphill
            value = value - jnp.where(where == 0, low * 0.5, 0.0)
            return value + jnp.where(where == rows - 1, high * 0.5, 0.0)

        for i in range(3):
            value = velocity[i, own]
            low, high = low_high(side, y_pair[6 + i, k : k + 1], y_next[6 + i, k : k + 1])
            around = velocity[i, across] + moving[6 + i] - 6.0 * value
            for ends in (y_ends(value, low, high, rows), z_ends(value)):
                around = around + ends[0] + ends[1]
            pull = total(i) + viscosity * around
            velocity_new[i, own] = value + time_step * occupied * pull / density
            displacement_grad[i, own] = -total(3 + i)


def finish_kernel(mine, other, g_in, gb_in, g_mid, gb_mid, g_out, gb_out, small):
    count, height, _ = mine.shape
    part = height - SMALL
    total = jnp.sum(jnp.square(mine[...])) + jnp.sum(jnp.square(other[...]))
    scale = lax.rsqrt(jnp.full((1, 1), total, f32) / NPARAM + norm_eps)
    half, index = lax.rem(lax.axis_index("gy"), 2), lax.axis_index("gx")
    for m in range(count):
        for ref, side in ((mine, half), (other, 1 - half)):
            chunk = side * count + (index ^ m)
            g_mid[pl.ds(pl.multiple_of(chunk * part, part), part), :] = ref[m, :part] * scale
            small[pl.ds(pl.multiple_of(chunk * SMALL, SMALL), SMALL), :] = ref[m, part:] * scale
    g_in[...] = small[:FEAT]
    gb_in[...] = small[10:11]
    g_out[...] = small[16 : 16 + OUT]
    gb_mid[...] = small[32:34]
    gb_out[...] = small[34:35, :OUT]


def shapes(*items):
    return [jax.ShapeDtypeStruct(item, f32) for item in items]


def stay(value):
    if value.size < 2:
        return value
    return pltpu.with_memory_space_constraint(value, pltpu.HBM)


def swap_next(value, axis):
    inner = lax.axis_size(axis) - 1
    return lax.ppermute(
        value, axis, [(i, i + 1 if i % 2 else i - 1) for i in range(1, inner)]
    )


def swap(value, axis, mask):
    return lax.ppermute(value, axis, [(i, i ^ mask) for i in range(lax.axis_size(axis))])


def body(
    material,
    phase,
    clock,
    displacement,
    velocity,
    cotangent,
    material_table,
    w_in,
    b_in,
    w_mid,
    b_mid,
    w_out,
    b_out,
):
    planes, rows, lanes = material.shape
    size = planes * rows
    nx, ny = lax.axis_size("gx"), lax.axis_size("gy")
    chunks = 2 * nx
    part = 2 * HID // chunks
    assert planes == 2 and chunks >= GROUPS and nx % 2 == ny % 2 == 0 and part % 8 == 0
    material = material.reshape(size, lanes)
    phase = phase.reshape(size, lanes)
    displacement = displacement.reshape(3, size, lanes)
    velocity = velocity.reshape(3, size, lanes)
    cotangent = cotangent.reshape(3, size, lanes)

    faces = pl.pallas_call(
        functools.partial(faces_kernel, rows),
        out_shape=shapes((6, rows, lanes), (9, rows, lanes), *[(9, 2, lanes)] * 2),
        in_specs=[HBM] * 5,
        out_specs=[VMEM] * 4,
        scratch_shapes=[
            pltpu.SMEM(material_table.shape, f32),
            pltpu.VMEM((size, lanes), jnp.int32),
            *[pltpu.VMEM((3, size, lanes), f32)] * 3,
            pltpu.SemaphoreType.DMA((5,)),
        ],
        compiler_params=pltpu.CompilerParams(vmem_limit_bytes=6 << 20),
        name="faces",
    )(*map(stay, (material_table, material, displacement, velocity, cotangent)))
    x_pair = swap(faces[0], "gx", 1)
    y_pair = swap(faces[2], "gy", 1)
    y_next = swap_next(faces[3], "gy")
    x_next = swap_next(faces[1], "gx")

    voxels = rows * lanes
    block = 4096
    while voxels % block:
        block //= 2
    handed = [
        ((2 * HID, HID), f32),
        ((16, HID), f32),
        ((16, HID), f32),
        ((2, HID, 128), f32),
        ((16, 128), f32),
        ((HID, 16), bf16),
        ((16, HID), bf16),
        ((2, HID, HID), bf16),
        ((16, HID), bf16),
        ((HID, 16), bf16),
        ((3, HID, 128), f32),
    ]

    def network(order, sources, near):
        outs = [jax.ShapeDtypeStruct(*item) for item in handed]
        if order:
            outs = shapes((chunks, part + SMALL, HID))
        return pl.pallas_call(
            functools.partial(network_kernel, order, rows, block),
            out_shape=shapes(
                (9 - 3 * order, rows, lanes), *[(6, 1 + order, lanes)] * 2, (6, rows, lanes)
            )
            + outs,
            in_specs=[HBM] * len(sources) + [VMEM] * len(near),
            out_specs=[VMEM] * (4 + len(outs)),
            scratch_shapes=[
                *[pltpu.SMEM(item.shape, f32) for item in sources[:3]],
                *[pltpu.VMEM(item.shape, item.dtype) for item in sources[3:]],
                pltpu.SemaphoreType.DMA((len(sources),)),
                *[pltpu.VMEM((lanes // 128, 16 * rows, 128), f32)] * 2,
                *[pltpu.VMEM((16, voxels), bf16)] * 2,
                *[pltpu.VMEM((16, voxels), f32)] * 2,
                pltpu.VMEM((128, HID), f32),
                *[pltpu.VMEM(*item) for item in handed[: 5 * order]],
            ],
            compiler_params=pltpu.CompilerParams(vmem_limit_bytes=36 << 20),
            cost_estimate=pl.CostEstimate(
                flops=6 * voxels * (HID * FEAT + 2 * HID * HID + OUT * HID),
                bytes_accessed=64 * voxels,
                transcendentals=3 * HID * voxels,
            ),
            name="network",
        )(*map(stay, sources), *near)

    common = [material_table, clock, b_out, material, phase, displacement, cotangent, w_mid]
    first = network(
        0,
        common + [w_in.T, b_in.reshape(1, HID), b_mid, w_out, velocity],
        [x_pair, y_pair, y_next],
    )
    sx_pair = swap(first[0], "gx", 1)
    second = network(1, common, [x_next, y_pair, y_next, *first[1:3], *first[4:]])
    sx_next = swap_next(second[0], "gx")

    half = lax.axis_index("gy") % 2
    index = lax.axis_index("gx")
    pile, sx_pair = lax.optimization_barrier((second[4], sx_pair))
    pile = pile.reshape(2, nx, part + SMALL, HID)
    kept = lax.dynamic_index_in_dim(pile, half, 0, keepdims=False)
    sent = lax.dynamic_index_in_dim(pile, 1 - half, 0, keepdims=False)
    kept, face = lax.optimization_barrier((kept + swap(sent, "gy", 1), second[2]))
    sy_next = swap_next(face, "gy")
    share = lax.dynamic_index_in_dim(kept, index, 0, keepdims=False)
    for m in range(1, nx):
        piece = lax.dynamic_index_in_dim(kept, index ^ m, 0, keepdims=False)
        share = share + swap(piece, "gx", m)
    share, face = lax.optimization_barrier((share, second[1]))
    sy_pair = swap(face, "gy", 1)
    mask = 2
    while mask < ny:
        share = share + swap(share, "gy", mask)
        if mask == 2:
            share, sx_next, sy_next = lax.optimization_barrier((share, sx_next, sy_next))
        mask *= 2
    share, sy_pair = lax.optimization_barrier((share, sy_pair))
    mine = jnp.stack([share] + [swap(share, "gx", m) for m in range(1, nx)])

    fields = pl.pallas_call(
        functools.partial(fields_kernel, rows),
        out_shape=shapes(*[(3, size, lanes)] * 2),
        in_specs=[SMEM] + [VMEM] * 13,
        out_specs=[VMEM] * 2,
        compiler_params=pltpu.CompilerParams(vmem_limit_bytes=6 << 20),
        name="fields",
    )(
        stay(material_table),
        stay(material),
        stay(velocity),
        first[0],
        second[0],
        first[3],
        second[3],
        x_next,
        y_pair,
        y_next,
        sx_pair,
        sx_next,
        sy_pair,
        sy_next,
    )
    mine, *fields = lax.optimization_barrier((mine, *fields))
    other = swap(mine, "gy", 1)
    done = pl.pallas_call(
        finish_kernel,
        out_shape=shapes((FEAT, HID), (1, HID), (2 * HID, HID), (2, HID), (OUT, HID), (1, OUT)),
        in_specs=[VMEM] * 2,
        out_specs=[VMEM] * 6,
        scratch_shapes=[pltpu.VMEM((chunks * SMALL, HID), f32)],
        compiler_params=pltpu.CompilerParams(vmem_limit_bytes=6 << 20),
        name="finish",
    )(mine, other)
    shape = (3, planes, rows, lanes)
    return (
        fields[0].reshape(shape),
        fields[1].reshape(shape),
        done[0].T,
        done[1].reshape(HID),
        done[2].reshape(2, HID, HID),
        done[3],
        done[4],
        done[5].reshape(OUT),
    )


def solution(mesh):
    in_specs = (
        P("gx", "gy", None),
        P("gx", "gy", None),
        P(),
        P(None, "gx", "gy", None),
        P(None, "gx", "gy", None),
        P(None, "gx", "gy", None),
        P(),
        P(),
        P(),
        P(),
        P(),
        P(),
        P(),
    )
    out_specs = (P(None, "gx", "gy", None), P(None, "gx", "gy", None), P(), P(), P(), P(), P(), P())
    return jax.shard_map(body, mesh=mesh, in_specs=in_specs, out_specs=out_specs, check_vma=False)
```

```python
import functools
import jax
import jax.numpy as jnp
from jax import lax
from jax.experimental import pallas as pl
from jax.experimental.pallas import tpu as pltpu
from jax.sharding import PartitionSpec as P

FEAT = 10
OUT = 9
HID = 256
PHASES = 8
NPARAM = 136713
SMALL = 8
GROUPS = 5

time_step = 0.25
viscosity = 0.2
norm_eps = 1e-06
two_pi = 6.283185307179586

bf16 = jnp.bfloat16
f32 = jnp.float32
VMEM = pl.BlockSpec(memory_space=pltpu.VMEM)
SMEM = pl.BlockSpec(memory_space=pltpu.SMEM)
HBM = pl.BlockSpec(memory_space=pltpu.HBM)


def fetch(sources, targets, sems):
    copies = [
        pltpu.make_async_copy(source, target, sems.at[k])
        for k, (source, target) in enumerate(zip(sources, targets))
    ]
    for copy in copies:
        copy.start()
    return copies


def pick(table, row, material):
    value = jnp.full(material.shape, table[row, 0], f32)
    for kind in range(1, table.shape[1]):
        value = jnp.where(material == kind, table[row, kind], value)
    return value


def step_factor(table, material):
    occupied = jnp.where(material > 0, 1.0, 0.0).astype(f32)
    return occupied, pick(table, 1, material)


def near_first():
    near = 1 - lax.rem(lax.axis_index("gx"), 2)
    return near, lax.rem(lax.axis_index("gy"), 2)


def y_ends(field, low, high, rows):
    where = lax.broadcasted_iota(jnp.int32, field.shape, 0)
    return (
        jnp.where(where == 0, low, pltpu.roll(field, 1, 0)),
        jnp.where(where == rows - 1, high, pltpu.roll(field, rows - 1, 0)),
    )


def z_ends(field):
    lanes = field.shape[1]
    where = lax.broadcasted_iota(jnp.int32, field.shape, 1)
    return (
        jnp.where(where == 0, 0.0, pltpu.roll(field, 1, 1)),
        jnp.where(where == lanes - 1, 0.0, pltpu.roll(field, lanes - 1, 1)),
    )


def half_diff(ends):
    return (ends[1] - ends[0]) * 0.5


def faces_kernel(rows, *refs):
    sources, outs, targets, sems = refs[:5], refs[5:9], refs[9:14], refs[14]
    copies = fetch(sources, targets, sems)
    near, side = near_first()
    for copy in copies:
        copy.wait()
    x_pair, x_next, y_pair, y_next = outs
    table, material, displacement, velocity, cotangent = targets
    for k, plane in enumerate((near, 1 - near)):
        own = pl.ds(pl.multiple_of(plane * rows, rows), rows)
        occupied, density = step_factor(table, material[own])
        for i in range(3):
            carried = time_step * occupied * cotangent[i, own] / density
            moving = velocity[i, own]
            for slot, field in ((i, displacement[i, own]), (3 + i, carried), (6 + i, moving)):
                if k:
                    x_next[slot] = field
                elif slot < 6:
                    x_pair[slot] = field
                y_pair[slot, k : k + 1] = jnp.where(side == 0, field[rows - 1 :], field[:1])
                y_next[slot, k : k + 1] = jnp.where(side == 0, field[:1], field[rows - 1 :])


def put_face(ref, base, slot, k, face):
    pieces = face.shape[1] // HID
    at = base + (2 * slot + k) * pieces
    for j in range(pieces):
        ref[at + j : at + j + 1] = face[:, j * HID : (j + 1) * HID]


def get_face(ref, base, slot, k, lanes):
    pieces = lanes // HID
    at = base + (2 * slot + k) * pieces
    return jnp.concatenate([ref[at + j : at + j + 1] for j in range(pieces)], 1)


def low_high(side, pair, following):
    return jnp.where(side == 0, following, pair), jnp.where(side == 0, pair, following)


def network_kernel(order, rows, block, *refs):
    sources, refs = refs[: 13 - order * 5], refs[13 - order * 5 :]
    (edge, y_pair, y_next), refs = refs[:3], refs[3:]
    if order:
        faces_first, given, refs = refs[:2], refs[2:13], refs[13:]
        (sx, s_next, rest, kept_half, sent), refs = refs[:5], refs[5:]
    else:
        (sx, s_pair, s_next, rest), kept, refs = refs[:4], refs[4:15], refs[15:]
    targets, sems, refs = refs[: len(sources)], refs[len(sources)], refs[len(sources) + 1 :]
    grid_in, grid_delta, feats, delta, net, back, wide, small, *refs = refs
    copies = fetch(sources, targets, sems)
    near, side = near_first()
    if order:
        acc_mid, acc_in, acc_out, acc_b, acc_bo = refs
        win, winT, wmidT, wout, woutT, bias = given[5:]
        for ref, source in zip(refs, given[:5]):
            ref[...] = source[...]
    else:
        acc_mid, acc_in, acc_out, acc_b, acc_bo = kept[:5]
        win, winT, wmidT, wout, woutT, bias = kept[5:]
        for ref in kept[:5]:
            ref[...] = jnp.zeros_like(ref)
    for copy in copies:
        copy.wait()
    table, clock, b_out, material, phase, displacement, cotangent, w_mid = targets[:8]
    lanes = material.shape[1]
    tiles = lanes // 128
    voxels = rows * lanes
    plane = 1 - near if order else near
    own = pl.ds(pl.multiple_of(plane * rows, rows), rows)
    across = pl.ds(pl.multiple_of((1 - plane) * rows, rows), rows)
    occupied, _ = step_factor(table, material[own])
    strength = occupied * pick(table, 0, material[own])

    if not order:
        w_inT, b_in, b_mid, w_out = targets[8:12]
        wide[...] = jnp.zeros_like(wide)
        wide[:FEAT] = w_inT[...].astype(f32)
        winT[...] = wide[:16].astype(bf16)
        win[...] = wide[...].T[:, :16].astype(bf16)
        wide[...] = jnp.zeros_like(wide)
        wide[:OUT] = w_out[...].astype(f32)
        wout[...] = wide[:16].astype(bf16)
        woutT[...] = wide[...].T[:, :16].astype(bf16)
        for k in range(2):
            wmidT[k] = w_mid[k].astype(f32).T.astype(bf16)
        for k, row in enumerate((b_in[...], b_mid[0:1], b_mid[1:2])):
            bias[k] = jnp.broadcast_to(row, (128, HID)).T

    def put(ref, slot, field):
        for t in range(tiles):
            ref[t, slot * rows : (slot + 1) * rows] = field[:, t * 128 : (t + 1) * 128]

    uphill = jnp.where(plane == 0, 0.5, -0.5)

    def strains(mine, other, slot):
        low, high = low_high(
            side, y_pair[slot, order : order + 1], y_next[slot, order : order + 1]
        )
        return (
            (other - edge[slot]) * uphill,
            half_diff(y_ends(mine, low, high, rows)),
            half_diff(z_ends(mine)),
        )

    def carried(rows_of, slot):
        full, thick = step_factor(table, material[rows_of])
        return time_step * full * cotangent[slot, rows_of] / thick

    for i in range(3):
        for j, value in enumerate(strains(displacement[i, own], displacement[i, across], i)):
            put(grid_in, 3 * i + j, value)
        for j, value in enumerate(strains(carried(own, i), carried(across, i), 3 + i)):
            put(grid_delta, 3 * i + j, strength * -value)
    put(grid_in, 9, jnp.sin(two_pi * phase[own].astype(f32) / PHASES + clock[0]))
    put(grid_in, 10, jnp.ones((rows, lanes), f32))
    for slot in range(11, 16):
        put(grid_in, slot, jnp.zeros((rows, lanes), f32))
    for slot in range(9, 16):
        put(grid_delta, slot, jnp.zeros((rows, lanes), f32))
    for r in range(rows):
        for t in range(tiles):
            at = slice((r * tiles + t) * 128, (r * tiles + t + 1) * 128)
            feats[:, at] = grid_in[t, pl.ds(r, 16, stride=rows), :].astype(bf16)
            delta[:, at] = grid_delta[t, pl.ds(r, 16, stride=rows), :].astype(bf16)

    rowid = lax.broadcasted_iota(jnp.int32, (16, 1), 0)
    bias_out = jnp.zeros((16, 1), f32)
    for k in range(OUT):
        bias_out = jnp.where(rowid == k, b_out[k], bias_out)

    def mul(a, b):
        return jnp.dot(a, b, preferred_element_type=f32)

    def mul_t(a, b):
        return lax.dot_general(a, b, (((1,), (1,)), ((), ())), preferred_element_type=f32)

    def lane_sum(value):
        total = value[:, :128].astype(f32)
        for k in range(1, block // 128):
            total = total + value[:, k * 128 : (k + 1) * 128].astype(f32)
        return total

    def slope(value):
        wider = value.astype(f32)
        return 1.0 - wider * wider

    def step(index, carry):
        at = pl.ds(pl.multiple_of(index * block, block), block)
        f, d = feats[:, at], delta[:, at]
        h1 = jnp.tanh(mul(win[...], f) + bias[0][:, :1]).astype(bf16)
        h2 = jnp.tanh(mul(w_mid[0], h1) + bias[1][:, :1]).astype(bf16)
        h3 = jnp.tanh(mul(w_mid[1], h2) + bias[2][:, :1]).astype(bf16)
        net[:, at] = mul(wout[...], h3) + bias_out
        acc_out[...] += mul_t(d, h3)
        acc_bo[...] += lane_sum(d)
        d3 = (mul(woutT[...], d) * slope(h3)).astype(bf16)
        acc_mid[HID:] += mul_t(d3, h2)
        acc_b[1] += lane_sum(d3)
        d2 = (mul(wmidT[1], d3) * slope(h2)).astype(bf16)
        acc_mid[:HID] += mul_t(d2, h1)
        acc_b[0] += lane_sum(d2)
        d1 = (mul(wmidT[0], d2) * slope(h1)).astype(bf16)
        acc_in[...] += mul_t(f, d1)
        back[:, at] = mul(winT[...], d1)
        return carry

    lax.fori_loop(0, voxels // block, step, 0)

    for r in range(rows):
        for t in range(tiles):
            at = slice((r * tiles + t) * 128, (r * tiles + t + 1) * 128)
            grid_in[t, pl.ds(r, 16, stride=rows), :] = net[:, at]
            grid_delta[t, pl.ds(r, 16, stride=rows), :] = back[:, at]

    def get(ref, slot):
        return jnp.concatenate(
            [ref[t, slot * rows : (slot + 1) * rows] for t in range(tiles)], axis=1
        )

    for base, ref, scale in ((0, grid_in, strength), (3, grid_delta, None)):
        for i in range(3):
            along = [get(ref, 3 * i + j) for j in range(3)]
            if scale is not None:
                along = [scale * item for item in along]
            slot = base + i
            sx[slot] = along[0]
            first, last = along[1][:1], along[1][rows - 1 :]
            to_pair = jnp.where(side == 0, last, first)
            to_next = jnp.where(side == 0, first, last)
            if order:
                tail = sent.shape[0] - s_next.shape[0]
                near_pair, near_next = (ref[slot] for ref in faces_first)
                put_face(sent, tail, slot, 0, near_pair)
                put_face(sent, tail, slot, 1, to_pair)
                put_face(s_next, 0, slot, 0, near_next)
                put_face(s_next, 0, slot, 1, to_next)
            else:
                s_pair[slot] = to_pair
                s_next[slot] = to_next
            rest[slot] = half_diff(y_ends(along[1], 0.0, 0.0, rows)) + half_diff(
                z_ends(along[2])
            )
    if not order:
        for i in range(3):
            sx[6 + i] = targets[12][i, own]
        return

    count = kept_half.shape[0]
    part = HID // count
    small[...] = jnp.zeros_like(small)
    small[:8] = acc_in[:8]
    small[8:16] = jnp.where(rowid[:8] < 3, acc_in[8:], 0.0)
    small[16:32] = acc_out[...]
    for k in range(2):
        small[32 + k : 33 + k] = jnp.sum(acc_b[k].T, axis=0, keepdims=True)
    wide[...] = jnp.zeros_like(wide)
    wide[:16, :128] = acc_bo[...]
    small[34:35, :128] = jnp.sum(wide[:, :128].T, axis=0, keepdims=True)
    half = lax.rem(lax.axis_index("gy"), 2)
    for c in range(count):
        mine, theirs = half * count + c, (1 - half) * count + c
        kept_half[c, :part] = acc_mid[pl.ds(pl.multiple_of(mine * part, part), part)]
        kept_half[c, part:] = small[pl.ds(pl.multiple_of(mine * SMALL, SMALL), SMALL)]
        at = c * (part + SMALL)
        sent[at : at + part] = acc_mid[pl.ds(pl.multiple_of(theirs * part, part), part)]
        at += part
        sent[at : at + SMALL] = small[pl.ds(pl.multiple_of(theirs * SMALL, SMALL), SMALL)]


def fields_kernel(
    rows,
    table,
    material,
    velocity,
    stress_near,
    stress_far,
    rest_near,
    rest_far,
    x_next,
    y_pair,
    y_next,
    sx_pair,
    sx_next,
    sy_pair,
    sy_next,
    velocity_new,
    displacement_grad,
):
    near, side = near_first()
    lanes = material.shape[1]
    where = lax.broadcasted_iota(jnp.int32, (rows, lanes), 0)
    for k, plane in enumerate((near, 1 - near)):
        own = pl.ds(pl.multiple_of(plane * rows, rows), rows)
        across = pl.ds(pl.multiple_of((1 - plane) * rows, rows), rows)
        occupied, density = step_factor(table, material[own])
        uphill = jnp.where(plane == 0, 0.5, -0.5)
        other, edge = (stress_near, sx_next) if k else (stress_far, sx_pair)
        moving, rest = (x_next, rest_far) if k else (sx_pair, rest_near)

        def total(slot):
            low, high = low_high(
                side,
                get_face(sy_pair, sy_pair.shape[0] - sy_next.shape[0], slot, k, lanes),
                get_face(sy_next, 0, slot, k, lanes),
            )
            value = rest[slot] + (other[slot] - edge[slot]) * uphill
            value = value - jnp.where(where == 0, low * 0.5, 0.0)
            return value + jnp.where(where == rows - 1, high * 0.5, 0.0)

        for i in range(3):
            value = velocity[i, own]
            low, high = low_high(side, y_pair[6 + i, k : k + 1], y_next[6 + i, k : k + 1])
            around = velocity[i, across] + moving[6 + i] - 6.0 * value
            for ends in (y_ends(value, low, high, rows), z_ends(value)):
                around = around + ends[0] + ends[1]
            pull = total(i) + viscosity * around
            velocity_new[i, own] = value + time_step * occupied * pull / density
            displacement_grad[i, own] = -total(3 + i)


def finish_kernel(mine, other, g_in, gb_in, g_mid, gb_mid, g_out, gb_out, small):
    count, height, _ = mine.shape
    part = height - SMALL
    total = jnp.sum(jnp.square(mine[...])) + jnp.sum(jnp.square(other[...]))
    scale = lax.rsqrt(jnp.full((1, 1), total, f32) / NPARAM + norm_eps)
    half, index = lax.rem(lax.axis_index("gy"), 2), lax.axis_index("gx")
    for m in range(count):
        for ref, side in ((mine, half), (other, 1 - half)):
            chunk = side * count + (index ^ m)
            g_mid[pl.ds(pl.multiple_of(chunk * part, part), part), :] = ref[m, :part] * scale
            small[pl.ds(pl.multiple_of(chunk * SMALL, SMALL), SMALL), :] = ref[m, part:] * scale
    g_in[...] = small[:FEAT]
    gb_in[...] = small[10:11]
    g_out[...] = small[16 : 16 + OUT]
    gb_mid[...] = small[32:34]
    gb_out[...] = small[34:35, :OUT]


def shapes(*items):
    return [jax.ShapeDtypeStruct(item, f32) for item in items]


def stay(value):
    if value.size < 2:
        return value
    return pltpu.with_memory_space_constraint(value, pltpu.HBM)


def swap_next(value, axis):
    inner = lax.axis_size(axis) - 1
    return lax.ppermute(
        value, axis, [(i, i + 1 if i % 2 else i - 1) for i in range(1, inner)]
    )


def swap(value, axis, mask):
    return lax.ppermute(value, axis, [(i, i ^ mask) for i in range(lax.axis_size(axis))])


def body(
    material,
    phase,
    clock,
    displacement,
    velocity,
    cotangent,
    material_table,
    w_in,
    b_in,
    w_mid,
    b_mid,
    w_out,
    b_out,
):
    planes, rows, lanes = material.shape
    size = planes * rows
    nx, ny = lax.axis_size("gx"), lax.axis_size("gy")
    chunks = 2 * nx
    part = 2 * HID // chunks
    face_rows = 12 * (lanes // HID)
    assert lanes % HID == 0 and ny & (ny - 1) == 0
    assert planes == 2 and chunks >= GROUPS and nx % 2 == ny % 2 == 0 and part % 8 == 0
    material = material.reshape(size, lanes)
    phase = phase.reshape(size, lanes)
    displacement = displacement.reshape(3, size, lanes)
    velocity = velocity.reshape(3, size, lanes)
    cotangent = cotangent.reshape(3, size, lanes)

    faces = pl.pallas_call(
        functools.partial(faces_kernel, rows),
        out_shape=shapes((6, rows, lanes), (9, rows, lanes), *[(9, 2, lanes)] * 2),
        in_specs=[HBM] * 5,
        out_specs=[VMEM] * 4,
        scratch_shapes=[
            pltpu.SMEM(material_table.shape, f32),
            pltpu.VMEM((size, lanes), jnp.int32),
            *[pltpu.VMEM((3, size, lanes), f32)] * 3,
            pltpu.SemaphoreType.DMA((5,)),
        ],
        compiler_params=pltpu.CompilerParams(vmem_limit_bytes=6 << 20),
        name="faces",
    )(*map(stay, (material_table, material, displacement, velocity, cotangent)))
    x_pair = swap(faces[0], "gx", 1)
    y_pair = swap(faces[2], "gy", 1)
    y_next = swap_next(faces[3], "gy")
    x_next = swap_next(faces[1], "gx")

    voxels = rows * lanes
    block = 4096
    while voxels % block:
        block //= 2
    handed = [
        ((2 * HID, HID), f32),
        ((16, HID), f32),
        ((16, HID), f32),
        ((2, HID, 128), f32),
        ((16, 128), f32),
        ((HID, 16), bf16),
        ((16, HID), bf16),
        ((2, HID, HID), bf16),
        ((16, HID), bf16),
        ((HID, 16), bf16),
        ((3, HID, 128), f32),
    ]

    def network(order, sources, near):
        outs = [jax.ShapeDtypeStruct(*item) for item in handed]
        faces_out = [(6, 1, lanes)] * 2
        if order:
            outs = shapes((nx, part + SMALL, HID), (nx * (part + SMALL) + face_rows, HID))
            faces_out = [(face_rows, HID)]
        return pl.pallas_call(
            functools.partial(network_kernel, order, rows, block),
            out_shape=shapes(
                (9 - 3 * order, rows, lanes), *faces_out, (6, rows, lanes)
            )
            + outs,
            in_specs=[HBM] * len(sources) + [VMEM] * len(near),
            out_specs=[VMEM] * (2 + len(faces_out) + len(outs)),
            scratch_shapes=[
                *[pltpu.SMEM(item.shape, f32) for item in sources[:3]],
                *[pltpu.VMEM(item.shape, item.dtype) for item in sources[3:]],
                pltpu.SemaphoreType.DMA((len(sources),)),
                *[pltpu.VMEM((lanes // 128, 16 * rows, 128), f32)] * 2,
                *[pltpu.VMEM((16, voxels), bf16)] * 2,
                *[pltpu.VMEM((16, voxels), f32)] * 2,
                pltpu.VMEM((128, HID), f32),
                pltpu.VMEM((chunks * SMALL, HID), f32),
                *[pltpu.VMEM(*item) for item in handed[: 5 * order]],
            ],
            compiler_params=pltpu.CompilerParams(vmem_limit_bytes=36 << 20),
            cost_estimate=pl.CostEstimate(
                flops=6 * voxels * (HID * FEAT + 2 * HID * HID + OUT * HID),
                bytes_accessed=64 * voxels,
                transcendentals=3 * HID * voxels,
            ),
            name="network",
        )(*map(stay, sources), *near)

    common = [material_table, clock, b_out, material, phase, displacement, cotangent, w_mid]
    first = network(
        0,
        common + [w_in.T, b_in.reshape(1, HID), b_mid, w_out, velocity],
        [x_pair, y_pair, y_next],
    )
    sx_pair = swap(first[0], "gx", 1)
    second = network(1, common, [x_next, y_pair, y_next, *first[1:3], *first[4:]])
    sx_next = swap_next(second[0], "gx")

    index = lax.axis_index("gx")
    sent, sx_pair = lax.optimization_barrier((second[4], sx_pair))
    sy_pair = swap(sent, "gy", 1)
    height = part + SMALL
    kept = second[3] + sy_pair[: nx * height].reshape(nx, height, HID)
    share = lax.dynamic_index_in_dim(kept, index, 0, keepdims=False)
    for m in range(1, nx):
        piece = lax.dynamic_index_in_dim(kept, index ^ m, 0, keepdims=False)
        share = share + swap(piece, "gx", m)
    share, face = lax.optimization_barrier((share, second[1]))
    sy_next = swap_next(face, "gy")
    mask = 2
    while mask < ny:
        share = share + swap(share, "gy", mask)
        if mask == 2:
            share, sx_next = lax.optimization_barrier((share, sx_next))
        mask *= 2
    share, sy_next = lax.optimization_barrier((share, sy_next))
    mine = jnp.stack([share] + [swap(share, "gx", m) for m in range(1, nx)])

    fields = pl.pallas_call(
        functools.partial(fields_kernel, rows),
        out_shape=shapes(*[(3, size, lanes)] * 2),
        in_specs=[SMEM] + [VMEM] * 13,
        out_specs=[VMEM] * 2,
        compiler_params=pltpu.CompilerParams(vmem_limit_bytes=6 << 20),
        name="fields",
    )(
        stay(material_table),
        stay(material),
        stay(velocity),
        first[0],
        second[0],
        first[3],
        second[2],
        x_next,
        y_pair,
        y_next,
        sx_pair,
        sx_next,
        sy_pair,
        sy_next,
    )
    mine, *fields = lax.optimization_barrier((mine, *fields))
    other = swap(mine, "gy", 1)
    done = pl.pallas_call(
        finish_kernel,
        out_shape=shapes((FEAT, HID), (1, HID), (2 * HID, HID), (2, HID), (OUT, HID), (1, OUT)),
        in_specs=[VMEM] * 2,
        out_specs=[VMEM] * 6,
        scratch_shapes=[pltpu.VMEM((chunks * SMALL, HID), f32)],
        compiler_params=pltpu.CompilerParams(vmem_limit_bytes=6 << 20),
        name="finish",
    )(mine, other)
    shape = (3, planes, rows, lanes)
    return (
        fields[0].reshape(shape),
        fields[1].reshape(shape),
        done[0].T,
        done[1].reshape(HID),
        done[2].reshape(2, HID, HID),
        done[3],
        done[4],
        done[5].reshape(OUT),
    )


def solution(mesh):
    in_specs = (
        P("gx", "gy", None),
        P("gx", "gy", None),
        P(),
        P(None, "gx", "gy", None),
        P(None, "gx", "gy", None),
        P(None, "gx", "gy", None),
        P(),
        P(),
        P(),
        P(),
        P(),
        P(),
        P(),
    )
    out_specs = (P(None, "gx", "gy", None), P(None, "gx", "gy", None), P(), P(), P(), P(), P(), P())
    return jax.shard_map(body, mesh=mesh, in_specs=in_specs, out_specs=out_specs, check_vma=False)
```

```python
import functools
import jax
import jax.numpy as jnp
from jax import lax
from jax.experimental import pallas as pl
from jax.experimental.pallas import tpu as pltpu
from jax.sharding import PartitionSpec as P

FEAT = 10
OUT = 9
HID = 256
PHASES = 8
NPARAM = 136713
SMALL = 8
GROUPS = 5

time_step = 0.25
viscosity = 0.2
norm_eps = 1e-06
two_pi = 6.283185307179586

bf16 = jnp.bfloat16
f32 = jnp.float32
VMEM = pl.BlockSpec(memory_space=pltpu.VMEM)
SMEM = pl.BlockSpec(memory_space=pltpu.SMEM)
HBM = pl.BlockSpec(memory_space=pltpu.HBM)


def fetch(sources, targets, sems):
    copies = [
        pltpu.make_async_copy(source, target, sems.at[k])
        for k, (source, target) in enumerate(zip(sources, targets))
    ]
    for copy in copies:
        copy.start()
    return copies


def pick(table, row, material):
    value = jnp.full(material.shape, table[row, 0], f32)
    for kind in range(1, table.shape[1]):
        value = jnp.where(material == kind, table[row, kind], value)
    return value


def step_factor(table, material):
    occupied = jnp.where(material > 0, 1.0, 0.0).astype(f32)
    return occupied, pick(table, 1, material)


def near_first():
    near = 1 - lax.rem(lax.axis_index("gx"), 2)
    return near, lax.rem(lax.axis_index("gy"), 2)


def y_ends(field, low, high, rows):
    where = lax.broadcasted_iota(jnp.int32, field.shape, 0)
    return (
        jnp.where(where == 0, low, pltpu.roll(field, 1, 0)),
        jnp.where(where == rows - 1, high, pltpu.roll(field, rows - 1, 0)),
    )


def z_ends(field):
    lanes = field.shape[1]
    where = lax.broadcasted_iota(jnp.int32, field.shape, 1)
    return (
        jnp.where(where == 0, 0.0, pltpu.roll(field, 1, 1)),
        jnp.where(where == lanes - 1, 0.0, pltpu.roll(field, lanes - 1, 1)),
    )


def half_diff(ends):
    return (ends[1] - ends[0]) * 0.5


def faces_kernel(rows, *refs):
    sources, outs, targets, sems = refs[:6], refs[6:12], refs[12:18], refs[18]
    copies = fetch(sources, targets, sems)
    near, side = near_first()
    for copy in copies:
        copy.wait()
    x_pair, x_next, y_pair, y_next, local, speed = outs
    table, material, phase, displacement, velocity, cotangent = targets
    for k, plane in enumerate((near, 1 - near)):
        own = pl.ds(pl.multiple_of(plane * rows, rows), rows)
        occupied, density = step_factor(table, material[own])
        local[k, 6] = occupied * pick(table, 0, material[own])
        local[k, 7] = two_pi * phase[own].astype(f32) / PHASES
        for i in range(3):
            carried = time_step * occupied * cotangent[i, own] / density
            moving = velocity[i, own]
            if not k:
                speed[i] = moving
            for slot, field in ((i, displacement[i, own]), (3 + i, carried), (6 + i, moving)):
                if slot < 6:
                    local[k, slot] = field
                if k:
                    x_next[slot] = field
                elif slot < 6:
                    x_pair[slot] = field
                y_pair[slot, k : k + 1] = jnp.where(side == 0, field[rows - 1 :], field[:1])
                y_next[slot, k : k + 1] = jnp.where(side == 0, field[:1], field[rows - 1 :])


def put_face(ref, base, slot, k, face):
    pieces = face.shape[1] // HID
    at = base + (2 * slot + k) * pieces
    for j in range(pieces):
        ref[at + j : at + j + 1] = face[:, j * HID : (j + 1) * HID]


def get_face(ref, base, slot, k, lanes):
    pieces = lanes // HID
    at = base + (2 * slot + k) * pieces
    return jnp.concatenate([ref[at + j : at + j + 1] for j in range(pieces)], 1)


def low_high(side, pair, following):
    return jnp.where(side == 0, following, pair), jnp.where(side == 0, pair, following)


def weights_kernel(*refs):
    sources, outs, refs = refs[:6], refs[7:15], refs[15:]
    b_out, w_inT, b_in, b_mid, w_out, sems, wide = refs
    win, winT, wmidT, wout, woutT, bias, w_mid, bias_out = outs
    for copy in fetch(sources, (b_out, w_inT, b_in, b_mid, w_out, w_mid), sems):
        copy.wait()
    rowid = lax.broadcasted_iota(jnp.int32, (16, 128), 0)
    wide[...] = jnp.zeros_like(wide)
    wide[:FEAT] = w_inT[...].astype(f32)
    winT[...] = wide[:16].astype(bf16)
    win[...] = wide[...].T[:, :16].astype(bf16)
    wide[...] = jnp.zeros_like(wide)
    wide[:OUT] = w_out[...].astype(f32)
    wout[...] = wide[:16].astype(bf16)
    woutT[...] = wide[...].T[:, :16].astype(bf16)
    for k in range(2):
        wmidT[k] = w_mid[k].astype(f32).T.astype(bf16)
    for k, row in enumerate((b_in[...], b_mid[0:1], b_mid[1:2])):
        bias[k] = jnp.broadcast_to(row, (128, HID)).T
    column = jnp.zeros((16, 128), f32)
    for k in range(OUT):
        column = jnp.where(rowid == k, b_out[k], column)
    bias_out[...] = column


def network_kernel(order, rows, block, *refs):
    clock, edge, y_pair, y_next, local, *refs = refs
    (win, winT, wmidT, wout, woutT, bias, w_mid, bias_out), refs = refs[:8], refs[8:]
    if order:
        faces_first, given, refs = refs[:2], refs[2:7], refs[7:]
        (sx, s_next, rest, kept_half, sent), refs = refs[:5], refs[5:]
    else:
        speed, sx, s_pair, s_next, rest, *refs = refs
        given, refs = refs[:5], refs[5:]
    grid_in, grid_delta, feats, delta, net, back, wide, small, *refs = refs
    near, side = near_first()
    if order:
        acc_mid, acc_in, acc_out, acc_b, acc_bo = refs
        for ref, source in zip(refs, given):
            ref[...] = source[...]
    else:
        acc_mid, acc_in, acc_out, acc_b, acc_bo = given
        for ref in given:
            ref[...] = jnp.zeros_like(ref)
    lanes = local.shape[3]
    tiles = lanes // 128
    voxels = rows * lanes
    plane = 1 - near if order else near
    strength = local[order, 6]

    def put(ref, slot, field):
        for t in range(tiles):
            ref[t, slot * rows : (slot + 1) * rows] = field[:, t * 128 : (t + 1) * 128]

    uphill = jnp.where(plane == 0, 0.5, -0.5)

    def strains(mine, other, slot):
        low, high = low_high(
            side, y_pair[slot, order : order + 1], y_next[slot, order : order + 1]
        )
        return (
            (other - edge[slot]) * uphill,
            half_diff(y_ends(mine, low, high, rows)),
            half_diff(z_ends(mine)),
        )

    for i in range(3):
        for j, value in enumerate(strains(local[order, i], local[1 - order, i], i)):
            put(grid_in, 3 * i + j, value)
        for j, value in enumerate(strains(local[order, 3 + i], local[1 - order, 3 + i], 3 + i)):
            put(grid_delta, 3 * i + j, strength * -value)
    put(grid_in, 9, jnp.sin(local[order, 7] + clock[0]))
    put(grid_in, 10, jnp.ones((rows, lanes), f32))
    for slot in range(11, 16):
        put(grid_in, slot, jnp.zeros((rows, lanes), f32))
    for slot in range(9, 16):
        put(grid_delta, slot, jnp.zeros((rows, lanes), f32))
    for r in range(rows):
        for t in range(tiles):
            at = slice((r * tiles + t) * 128, (r * tiles + t + 1) * 128)
            feats[:, at] = grid_in[t, pl.ds(r, 16, stride=rows), :].astype(bf16)
            delta[:, at] = grid_delta[t, pl.ds(r, 16, stride=rows), :].astype(bf16)

    rowid = lax.broadcasted_iota(jnp.int32, (16, 128), 0)

    def mul(a, b):
        return jnp.dot(a, b, preferred_element_type=f32)

    def mul_t(a, b):
        return lax.dot_general(a, b, (((1,), (1,)), ((), ())), preferred_element_type=f32)

    def lane_sum(value):
        total = value[:, :128].astype(f32)
        for k in range(1, block // 128):
            total = total + value[:, k * 128 : (k + 1) * 128].astype(f32)
        return total

    def slope(value):
        wider = value.astype(f32)
        return 1.0 - wider * wider

    def step(index, carry):
        at = pl.ds(pl.multiple_of(index * block, block), block)
        f, d = feats[:, at], delta[:, at]
        h1 = jnp.tanh(mul(win[...], f) + bias[0][:, :1]).astype(bf16)
        h2 = jnp.tanh(mul(w_mid[0], h1) + bias[1][:, :1]).astype(bf16)
        h3 = jnp.tanh(mul(w_mid[1], h2) + bias[2][:, :1]).astype(bf16)
        net[:, at] = mul(wout[...], h3) + bias_out[:, :1]
        acc_out[...] += mul_t(d, h3)
        acc_bo[...] += lane_sum(d)
        d3 = (mul(woutT[...], d) * slope(h3)).astype(bf16)
        acc_mid[HID:] += mul_t(d3, h2)
        acc_b[1] += lane_sum(d3)
        d2 = (mul(wmidT[1], d3) * slope(h2)).astype(bf16)
        acc_mid[:HID] += mul_t(d2, h1)
        acc_b[0] += lane_sum(d2)
        d1 = (mul(wmidT[0], d2) * slope(h1)).astype(bf16)
        acc_in[...] += mul_t(f, d1)
        back[:, at] = mul(winT[...], d1)
        return carry

    lax.fori_loop(0, voxels // block, step, 0)

    for r in range(rows):
        for t in range(tiles):
            at = slice((r * tiles + t) * 128, (r * tiles + t + 1) * 128)
            grid_in[t, pl.ds(r, 16, stride=rows), :] = net[:, at]
            grid_delta[t, pl.ds(r, 16, stride=rows), :] = back[:, at]

    def get(ref, slot):
        return jnp.concatenate(
            [ref[t, slot * rows : (slot + 1) * rows] for t in range(tiles)], axis=1
        )

    for base, ref, scale in ((0, grid_in, strength), (3, grid_delta, None)):
        for i in range(3):
            along = [get(ref, 3 * i + j) for j in range(3)]
            if scale is not None:
                along = [scale * item for item in along]
            slot = base + i
            sx[slot] = along[0]
            first, last = along[1][:1], along[1][rows - 1 :]
            to_pair = jnp.where(side == 0, last, first)
            to_next = jnp.where(side == 0, first, last)
            if order:
                tail = sent.shape[0] - s_next.shape[0]
                near_pair, near_next = (ref[slot] for ref in faces_first)
                put_face(sent, tail, slot, 0, near_pair)
                put_face(sent, tail, slot, 1, to_pair)
                put_face(s_next, 0, slot, 0, near_next)
                put_face(s_next, 0, slot, 1, to_next)
            else:
                s_pair[slot] = to_pair
                s_next[slot] = to_next
            rest[slot] = half_diff(y_ends(along[1], 0.0, 0.0, rows)) + half_diff(
                z_ends(along[2])
            )
    if not order:
        for i in range(3):
            sx[6 + i] = speed[i]
        return

    count = kept_half.shape[0]
    part = HID // count
    small[...] = jnp.zeros_like(small)
    small[:8] = acc_in[:8]
    small[8:16] = jnp.where(rowid[:8, :1] < 3, acc_in[8:], 0.0)
    small[16:32] = acc_out[...]
    for k in range(2):
        small[32 + k : 33 + k] = jnp.sum(acc_b[k].T, axis=0, keepdims=True)
    wide[...] = jnp.zeros_like(wide)
    wide[:16, :128] = acc_bo[...]
    small[34:35, :128] = jnp.sum(wide[:, :128].T, axis=0, keepdims=True)
    half = lax.rem(lax.axis_index("gy"), 2)
    for c in range(count):
        mine, theirs = half * count + c, (1 - half) * count + c
        kept_half[c, :part] = acc_mid[pl.ds(pl.multiple_of(mine * part, part), part)]
        kept_half[c, part:] = small[pl.ds(pl.multiple_of(mine * SMALL, SMALL), SMALL)]
        at = c * (part + SMALL)
        sent[at : at + part] = acc_mid[pl.ds(pl.multiple_of(theirs * part, part), part)]
        at += part
        sent[at : at + SMALL] = small[pl.ds(pl.multiple_of(theirs * SMALL, SMALL), SMALL)]


def fields_kernel(
    rows,
    table,
    material,
    velocity,
    stress_near,
    stress_far,
    rest_near,
    rest_far,
    x_next,
    y_pair,
    y_next,
    sx_pair,
    sx_next,
    sy_pair,
    sy_next,
    velocity_new,
    displacement_grad,
):
    near, side = near_first()
    lanes = material.shape[1]
    where = lax.broadcasted_iota(jnp.int32, (rows, lanes), 0)
    for k, plane in enumerate((near, 1 - near)):
        own = pl.ds(pl.multiple_of(plane * rows, rows), rows)
        across = pl.ds(pl.multiple_of((1 - plane) * rows, rows), rows)
        occupied, density = step_factor(table, material[own])
        uphill = jnp.where(plane == 0, 0.5, -0.5)
        other, edge = (stress_near, sx_next) if k else (stress_far, sx_pair)
        moving, rest = (x_next, rest_far) if k else (sx_pair, rest_near)

        def total(slot):
            low, high = low_high(
                side,
                get_face(sy_pair, sy_pair.shape[0] - sy_next.shape[0], slot, k, lanes),
                get_face(sy_next, 0, slot, k, lanes),
            )
            value = rest[slot] + (other[slot] - edge[slot]) * uphill
            value = value - jnp.where(where == 0, low * 0.5, 0.0)
            return value + jnp.where(where == rows - 1, high * 0.5, 0.0)

        for i in range(3):
            value = velocity[i, own]
            low, high = low_high(side, y_pair[6 + i, k : k + 1], y_next[6 + i, k : k + 1])
            around = velocity[i, across] + moving[6 + i] - 6.0 * value
            for ends in (y_ends(value, low, high, rows), z_ends(value)):
                around = around + ends[0] + ends[1]
            pull = total(i) + viscosity * around
            velocity_new[i, own] = value + time_step * occupied * pull / density
            displacement_grad[i, own] = -total(3 + i)


def finish_kernel(mine, other, g_in, gb_in, g_mid, gb_mid, g_out, gb_out, small):
    count, height, _ = mine.shape
    part = height - SMALL
    total = jnp.sum(jnp.square(mine[...])) + jnp.sum(jnp.square(other[...]))
    scale = lax.rsqrt(jnp.full((1, 1), total, f32) / NPARAM + norm_eps)
    half, index = lax.rem(lax.axis_index("gy"), 2), lax.axis_index("gx")
    for m in range(count):
        for ref, side in ((mine, half), (other, 1 - half)):
            chunk = side * count + (index ^ m)
            g_mid[pl.ds(pl.multiple_of(chunk * part, part), part), :] = ref[m, :part] * scale
            small[pl.ds(pl.multiple_of(chunk * SMALL, SMALL), SMALL), :] = ref[m, part:] * scale
    g_in[...] = small[:FEAT]
    gb_in[...] = small[10:11]
    g_out[...] = small[16 : 16 + OUT]
    gb_mid[...] = small[32:34]
    gb_out[...] = small[34:35, :OUT]


def shapes(*items):
    return [jax.ShapeDtypeStruct(item, f32) for item in items]


def stay(value):
    if value.size < 2:
        return value
    return pltpu.with_memory_space_constraint(value, pltpu.HBM)


def swap_next(value, axis):
    inner = lax.axis_size(axis) - 1
    return lax.ppermute(
        value, axis, [(i, i + 1 if i % 2 else i - 1) for i in range(1, inner)]
    )


def swap(value, axis, mask):
    return lax.ppermute(value, axis, [(i, i ^ mask) for i in range(lax.axis_size(axis))])


def body(
    material,
    phase,
    clock,
    displacement,
    velocity,
    cotangent,
    material_table,
    w_in,
    b_in,
    w_mid,
    b_mid,
    w_out,
    b_out,
):
    planes, rows, lanes = material.shape
    size = planes * rows
    nx, ny = lax.axis_size("gx"), lax.axis_size("gy")
    chunks = 2 * nx
    part = 2 * HID // chunks
    face_rows = 12 * (lanes // HID)
    assert lanes % HID == 0 and ny & (ny - 1) == 0
    assert planes == 2 and chunks >= GROUPS and nx % 2 == ny % 2 == 0 and part % 8 == 0
    material = material.reshape(size, lanes)
    phase = phase.reshape(size, lanes)
    displacement = displacement.reshape(3, size, lanes)
    velocity = velocity.reshape(3, size, lanes)
    cotangent = cotangent.reshape(3, size, lanes)

    faces = pl.pallas_call(
        functools.partial(faces_kernel, rows),
        out_shape=shapes(
            (6, rows, lanes),
            (9, rows, lanes),
            *[(9, 2, lanes)] * 2,
            (2, 8, rows, lanes),
            (3, rows, lanes),
        ),
        in_specs=[HBM] * 6,
        out_specs=[VMEM] * 6,
        scratch_shapes=[
            pltpu.SMEM(material_table.shape, f32),
            *[pltpu.VMEM((size, lanes), jnp.int32)] * 2,
            *[pltpu.VMEM((3, size, lanes), f32)] * 3,
            pltpu.SemaphoreType.DMA((6,)),
        ],
        compiler_params=pltpu.CompilerParams(vmem_limit_bytes=6 << 20),
        name="faces",
    )(*map(stay, (material_table, material, phase, displacement, velocity, cotangent)))
    x_pair = swap(faces[0], "gx", 1)
    y_pair = swap(faces[2], "gy", 1)
    y_next = swap_next(faces[3], "gy")
    x_next = swap_next(faces[1], "gx")

    voxels = rows * lanes
    block = 4096
    while voxels % block:
        block //= 2
    handed = [
        ((2 * HID, HID), f32),
        ((16, HID), f32),
        ((16, HID), f32),
        ((2, HID, 128), f32),
        ((16, 128), f32),
    ]
    ready = [
        ((HID, 16), bf16),
        ((16, HID), bf16),
        ((2, HID, HID), bf16),
        ((16, HID), bf16),
        ((HID, 16), bf16),
        ((3, HID, 128), f32),
        ((2, HID, HID), bf16),
        ((16, 128), f32),
    ]
    weights = pl.pallas_call(
        weights_kernel,
        out_shape=[jax.ShapeDtypeStruct(*item) for item in ready],
        in_specs=[HBM] * 6 + [VMEM],
        out_specs=[VMEM] * 8,
        scratch_shapes=[
            pltpu.SMEM(b_out.shape, f32),
            pltpu.VMEM((FEAT, HID), bf16),
            pltpu.VMEM((1, HID), f32),
            pltpu.VMEM((2, HID), f32),
            pltpu.VMEM((OUT, HID), bf16),
            pltpu.SemaphoreType.DMA((6,)),
            pltpu.VMEM((128, HID), f32),
        ],
        compiler_params=pltpu.CompilerParams(vmem_limit_bytes=6 << 20),
        name="weights",
    )(*map(stay, (b_out, w_in.T, b_in.reshape(1, HID), b_mid, w_out, w_mid)), faces[5])

    def network(order, near):
        outs = [jax.ShapeDtypeStruct(*item) for item in handed]
        faces_out = [(6, 1, lanes)] * 2
        if order:
            outs = shapes((nx, part + SMALL, HID), (nx * (part + SMALL) + face_rows, HID))
            faces_out = [(face_rows, HID)]
        return pl.pallas_call(
            functools.partial(network_kernel, order, rows, block),
            out_shape=shapes(
                (9 - 3 * order, rows, lanes), *faces_out, (6, rows, lanes)
            )
            + outs,
            in_specs=[SMEM] + [VMEM] * len(near),
            out_specs=[VMEM] * (2 + len(faces_out) + len(outs)),
            scratch_shapes=[
                *[pltpu.VMEM((lanes // 128, 16 * rows, 128), f32)] * 2,
                *[pltpu.VMEM((16, voxels), bf16)] * 2,
                *[pltpu.VMEM((16, voxels), f32)] * 2,
                pltpu.VMEM((128, HID), f32),
                pltpu.VMEM((chunks * SMALL, HID), f32),
                *[pltpu.VMEM(*item) for item in handed[: 5 * order]],
            ],
            compiler_params=pltpu.CompilerParams(vmem_limit_bytes=36 << 20),
            cost_estimate=pl.CostEstimate(
                flops=6 * voxels * (HID * FEAT + 2 * HID * HID + OUT * HID),
                bytes_accessed=64 * voxels,
                transcendentals=3 * HID * voxels,
            ),
            name="network",
        )(clock, *near)

    first = network(0, [x_pair, y_pair, y_next, faces[4], *weights, faces[5]])
    sx_pair = swap(first[0], "gx", 1)
    second = network(1, [x_next, y_pair, y_next, faces[4], *weights, *first[1:3], *first[4:]])
    sx_next = swap_next(second[0], "gx")

    index = lax.axis_index("gx")
    sent, sx_pair = lax.optimization_barrier((second[4], sx_pair))
    sy_pair = swap(sent, "gy", 1)
    height = part + SMALL
    kept = second[3] + sy_pair[: nx * height].reshape(nx, height, HID)
    share = lax.dynamic_index_in_dim(kept, index, 0, keepdims=False)
    for m in range(1, nx):
        piece = lax.dynamic_index_in_dim(kept, index ^ m, 0, keepdims=False)
        share = share + swap(piece, "gx", m)
    share, face = lax.optimization_barrier((share, second[1]))
    sy_next = swap_next(face, "gy")
    mask = 2
    while mask < ny:
        share = share + swap(share, "gy", mask)
        if mask == 2:
            share, sx_next = lax.optimization_barrier((share, sx_next))
        mask *= 2
    share, sy_next = lax.optimization_barrier((share, sy_next))
    mine = jnp.stack([share] + [swap(share, "gx", m) for m in range(1, nx)])

    fields = pl.pallas_call(
        functools.partial(fields_kernel, rows),
        out_shape=shapes(*[(3, size, lanes)] * 2),
        in_specs=[SMEM] + [VMEM] * 13,
        out_specs=[VMEM] * 2,
        compiler_params=pltpu.CompilerParams(vmem_limit_bytes=6 << 20),
        name="fields",
    )(
        stay(material_table),
        stay(material),
        stay(velocity),
        first[0],
        second[0],
        first[3],
        second[2],
        x_next,
        y_pair,
        y_next,
        sx_pair,
        sx_next,
        sy_pair,
        sy_next,
    )
    mine, *fields = lax.optimization_barrier((mine, *fields))
    other = swap(mine, "gy", 1)
    done = pl.pallas_call(
        finish_kernel,
        out_shape=shapes((FEAT, HID), (1, HID), (2 * HID, HID), (2, HID), (OUT, HID), (1, OUT)),
        in_specs=[VMEM] * 2,
        out_specs=[VMEM] * 6,
        scratch_shapes=[pltpu.VMEM((chunks * SMALL, HID), f32)],
        compiler_params=pltpu.CompilerParams(vmem_limit_bytes=6 << 20),
        name="finish",
    )(mine, other)
    shape = (3, planes, rows, lanes)
    return (
        fields[0].reshape(shape),
        fields[1].reshape(shape),
        done[0].T,
        done[1].reshape(HID),
        done[2].reshape(2, HID, HID),
        done[3],
        done[4],
        done[5].reshape(OUT),
    )


def solution(mesh):
    in_specs = (
        P("gx", "gy", None),
        P("gx", "gy", None),
        P(),
        P(None, "gx", "gy", None),
        P(None, "gx", "gy", None),
        P(None, "gx", "gy", None),
        P(),
        P(),
        P(),
        P(),
        P(),
        P(),
        P(),
    )
    out_specs = (P(None, "gx", "gy", None), P(None, "gx", "gy", None), P(), P(), P(), P(), P(), P())
    return jax.shard_map(body, mesh=mesh, in_specs=in_specs, out_specs=out_specs, check_vma=False)
```

```python
import functools
import jax
import jax.numpy as jnp
from jax import lax
from jax.experimental import pallas as pl
from jax.experimental.pallas import tpu as pltpu
from jax.sharding import PartitionSpec as P

FEAT = 10
OUT = 9
HID = 256
PHASES = 8
NPARAM = 136713
SMALL = 8
GROUPS = 5

time_step = 0.25
viscosity = 0.2
norm_eps = 1e-06
two_pi = 6.283185307179586

bf16 = jnp.bfloat16
f32 = jnp.float32
VMEM = pl.BlockSpec(memory_space=pltpu.VMEM)
SMEM = pl.BlockSpec(memory_space=pltpu.SMEM)
HBM = pl.BlockSpec(memory_space=pltpu.HBM)


def fetch(sources, targets, sems):
    copies = [
        pltpu.make_async_copy(source, target, sems.at[k])
        for k, (source, target) in enumerate(zip(sources, targets))
    ]
    for copy in copies:
        copy.start()
    return copies


def pick(table, row, material):
    value = jnp.full(material.shape, table[row, 0], f32)
    for kind in range(1, table.shape[1]):
        value = jnp.where(material == kind, table[row, kind], value)
    return value


def step_factor(table, material):
    occupied = jnp.where(material > 0, 1.0, 0.0).astype(f32)
    return occupied, pick(table, 1, material)


def near_first():
    near = 1 - lax.rem(lax.axis_index("gx"), 2)
    return near, lax.rem(lax.axis_index("gy"), 2)


def y_ends(field, low, high, rows):
    where = lax.broadcasted_iota(jnp.int32, field.shape, 0)
    return (
        jnp.where(where == 0, low, pltpu.roll(field, 1, 0)),
        jnp.where(where == rows - 1, high, pltpu.roll(field, rows - 1, 0)),
    )


def z_ends(field):
    lanes = field.shape[1]
    where = lax.broadcasted_iota(jnp.int32, field.shape, 1)
    return (
        jnp.where(where == 0, 0.0, pltpu.roll(field, 1, 1)),
        jnp.where(where == lanes - 1, 0.0, pltpu.roll(field, lanes - 1, 1)),
    )


def half_diff(ends):
    return (ends[1] - ends[0]) * 0.5


def faces_kernel(rows, *refs):
    sources, outs, targets, sems = refs[:6], refs[6:12], refs[12:18], refs[18]
    copies = fetch(sources, targets, sems)
    near, side = near_first()
    for copy in copies:
        copy.wait()
    x_pair, x_next, y_pair, y_next, local, speed = outs
    table, material, phase, displacement, velocity, cotangent = targets
    for k, plane in enumerate((near, 1 - near)):
        own = pl.ds(pl.multiple_of(plane * rows, rows), rows)
        occupied, density = step_factor(table, material[own])
        local[k, 6] = occupied * pick(table, 0, material[own])
        local[k, 7] = two_pi * phase[own].astype(f32) / PHASES
        for i in range(3):
            carried = time_step * occupied * cotangent[i, own] / density
            moving = velocity[i, own]
            if not k:
                speed[i] = moving
            for slot, field in ((i, displacement[i, own]), (3 + i, carried), (6 + i, moving)):
                if slot < 6:
                    local[k, slot] = field
                if k:
                    x_next[slot] = field
                elif slot < 6:
                    x_pair[slot] = field
                y_pair[slot, k : k + 1] = jnp.where(side == 0, field[rows - 1 :], field[:1])
                y_next[slot, k : k + 1] = jnp.where(side == 0, field[:1], field[rows - 1 :])


def put_face(ref, base, slot, k, face):
    pieces = face.shape[1] // HID
    at = base + (2 * slot + k) * pieces
    for j in range(pieces):
        ref[at + j : at + j + 1] = face[:, j * HID : (j + 1) * HID]


def get_face(ref, base, slot, k, lanes):
    pieces = lanes // HID
    at = base + (2 * slot + k) * pieces
    return jnp.concatenate([ref[at + j : at + j + 1] for j in range(pieces)], 1)


def low_high(side, pair, following):
    return jnp.where(side == 0, following, pair), jnp.where(side == 0, pair, following)


def weights_kernel(*refs):
    sources, outs, refs = refs[:6], refs[7:15], refs[15:]
    b_out, w_inT, b_in, b_mid, w_out, sems, wide = refs
    win, winT, wmidT, wout, woutT, bias, w_mid, bias_out = outs
    for copy in fetch(sources, (b_out, w_inT, b_in, b_mid, w_out, w_mid), sems):
        copy.wait()
    rowid = lax.broadcasted_iota(jnp.int32, (16, 128), 0)
    wide[...] = jnp.zeros_like(wide)
    wide[:FEAT] = w_inT[...].astype(f32)
    winT[...] = wide[:16].astype(bf16)
    win[...] = wide[...].T[:, :16].astype(bf16)
    wide[...] = jnp.zeros_like(wide)
    wide[:OUT] = w_out[...].astype(f32)
    wout[...] = wide[:16].astype(bf16)
    woutT[...] = wide[...].T[:, :16].astype(bf16)
    for k in range(2):
        wmidT[k] = w_mid[k].astype(f32).T.astype(bf16)
    for k, row in enumerate((b_in[...], b_mid[0:1], b_mid[1:2])):
        bias[k] = jnp.broadcast_to(row, (128, HID)).T
    column = jnp.zeros((16, 128), f32)
    for k in range(OUT):
        column = jnp.where(rowid == k, b_out[k], column)
    bias_out[...] = column


def network_kernel(order, rows, block, *refs):
    clock, edge, y_pair, y_next, local, *refs = refs
    (win, winT, wmidT, wout, woutT, bias, w_mid, bias_out), refs = refs[:8], refs[8:]
    if order:
        faces_first, given, refs = refs[:2], refs[2:7], refs[7:]
        (sx, s_next, rest, kept_half, sent), refs = refs[:5], refs[5:]
    else:
        speed, sx, s_pair, s_next, rest, *refs = refs
        given, refs = refs[:5], refs[5:]
    grid_in, grid_delta, feats, delta, net, back, wide, small, *refs = refs
    near, side = near_first()
    if order:
        acc_mid, acc_in, acc_out, acc_b, acc_bo = refs
        for ref, source in zip(refs, given):
            ref[...] = source[...]
    else:
        acc_mid, acc_in, acc_out, acc_b, acc_bo = given
        for ref in given:
            ref[...] = jnp.zeros_like(ref)
    lanes = local.shape[3]
    tiles = lanes // 128
    voxels = rows * lanes
    plane = 1 - near if order else near
    strength = local[order, 6]

    def put(ref, slot, field):
        for t in range(tiles):
            ref[t, slot * rows : (slot + 1) * rows] = field[:, t * 128 : (t + 1) * 128]

    uphill = jnp.where(plane == 0, 0.5, -0.5)

    def strains(mine, other, slot):
        low, high = low_high(
            side, y_pair[slot, order : order + 1], y_next[slot, order : order + 1]
        )
        return (
            (other - edge[slot]) * uphill,
            half_diff(y_ends(mine, low, high, rows)),
            half_diff(z_ends(mine)),
        )

    for i in range(3):
        for j, value in enumerate(strains(local[order, i], local[1 - order, i], i)):
            put(grid_in, 3 * i + j, value)
        for j, value in enumerate(strains(local[order, 3 + i], local[1 - order, 3 + i], 3 + i)):
            put(grid_delta, 3 * i + j, strength * -value)
    put(grid_in, 9, jnp.sin(local[order, 7] + clock[0]))
    put(grid_in, 10, jnp.ones((rows, lanes), f32))
    for slot in range(11, 16):
        put(grid_in, slot, jnp.zeros((rows, lanes), f32))
    for slot in range(9, 16):
        put(grid_delta, slot, jnp.zeros((rows, lanes), f32))
    for r in range(rows):
        for t in range(tiles):
            at = slice((r * tiles + t) * 128, (r * tiles + t + 1) * 128)
            feats[:, at] = grid_in[t, pl.ds(r, 16, stride=rows), :].astype(bf16)
            delta[:, at] = grid_delta[t, pl.ds(r, 16, stride=rows), :].astype(bf16)

    rowid = lax.broadcasted_iota(jnp.int32, (16, 128), 0)

    def mul(a, b):
        return jnp.dot(a, b, preferred_element_type=f32)

    def mul_t(a, b):
        return lax.dot_general(a, b, (((1,), (1,)), ((), ())), preferred_element_type=f32)

    def lane_sum(value):
        total = value[:, :128].astype(f32)
        for k in range(1, block // 128):
            total = total + value[:, k * 128 : (k + 1) * 128].astype(f32)
        return total

    def slope(value):
        wider = value.astype(f32)
        return 1.0 - wider * wider

    def step(index, carry):
        at = pl.ds(pl.multiple_of(index * block, block), block)
        f, d = feats[:, at], delta[:, at]
        h1 = jnp.tanh(mul(win[...], f) + bias[0][:, :1]).astype(bf16)
        h2 = jnp.tanh(mul(w_mid[0], h1) + bias[1][:, :1]).astype(bf16)
        h3 = jnp.tanh(mul(w_mid[1], h2) + bias[2][:, :1]).astype(bf16)
        net[:, at] = mul(wout[...], h3) + bias_out[:, :1]
        acc_out[...] += mul_t(d, h3)
        acc_bo[...] += lane_sum(d)
        d3 = (mul(woutT[...], d) * slope(h3)).astype(bf16)
        acc_mid[HID:] += mul_t(d3, h2)
        acc_b[1] += lane_sum(d3)
        d2 = (mul(wmidT[1], d3) * slope(h2)).astype(bf16)
        acc_mid[:HID] += mul_t(d2, h1)
        acc_b[0] += lane_sum(d2)
        d1 = (mul(wmidT[0], d2) * slope(h1)).astype(bf16)
        acc_in[...] += mul_t(f, d1)
        back[:, at] = mul(winT[...], d1)
        return carry

    lax.fori_loop(0, voxels // block, step, 0, unroll=2)

    for r in range(rows):
        for t in range(tiles):
            at = slice((r * tiles + t) * 128, (r * tiles + t + 1) * 128)
            grid_in[t, pl.ds(r, 16, stride=rows), :] = net[:, at]
            grid_delta[t, pl.ds(r, 16, stride=rows), :] = back[:, at]

    def get(ref, slot):
        return jnp.concatenate(
            [ref[t, slot * rows : (slot + 1) * rows] for t in range(tiles)], axis=1
        )

    for base, ref, scale in ((0, grid_in, strength), (3, grid_delta, None)):
        for i in range(3):
            along = [get(ref, 3 * i + j) for j in range(3)]
            if scale is not None:
                along = [scale * item for item in along]
            slot = base + i
            sx[slot] = along[0]
            first, last = along[1][:1], along[1][rows - 1 :]
            to_pair = jnp.where(side == 0, last, first)
            to_next = jnp.where(side == 0, first, last)
            if order:
                tail = sent.shape[0] - s_next.shape[0]
                near_pair, near_next = (ref[slot] for ref in faces_first)
                put_face(sent, tail, slot, 0, near_pair)
                put_face(sent, tail, slot, 1, to_pair)
                put_face(s_next, 0, slot, 0, near_next)
                put_face(s_next, 0, slot, 1, to_next)
            else:
                s_pair[slot] = to_pair
                s_next[slot] = to_next
            rest[slot] = half_diff(y_ends(along[1], 0.0, 0.0, rows)) + half_diff(
                z_ends(along[2])
            )
    if not order:
        for i in range(3):
            sx[6 + i] = speed[i]
        return

    count = kept_half.shape[0]
    part = HID // count
    small[...] = jnp.zeros_like(small)
    small[:8] = acc_in[:8]
    small[8:16] = jnp.where(rowid[:8, :1] < 3, acc_in[8:], 0.0)
    small[16:32] = acc_out[...]
    for k in range(2):
        small[32 + k : 33 + k] = jnp.sum(acc_b[k].T, axis=0, keepdims=True)
    wide[...] = jnp.zeros_like(wide)
    wide[:16, :128] = acc_bo[...]
    small[34:35, :128] = jnp.sum(wide[:, :128].T, axis=0, keepdims=True)
    half = lax.rem(lax.axis_index("gy"), 2)
    for c in range(count):
        mine, theirs = half * count + c, (1 - half) * count + c
        kept_half[c, :part] = acc_mid[pl.ds(pl.multiple_of(mine * part, part), part)]
        kept_half[c, part:] = small[pl.ds(pl.multiple_of(mine * SMALL, SMALL), SMALL)]
        at = c * (part + SMALL)
        sent[at : at + part] = acc_mid[pl.ds(pl.multiple_of(theirs * part, part), part)]
        at += part
        sent[at : at + SMALL] = small[pl.ds(pl.multiple_of(theirs * SMALL, SMALL), SMALL)]


def fields_kernel(
    rows,
    table,
    material,
    velocity,
    stress_near,
    stress_far,
    rest_near,
    rest_far,
    x_next,
    y_pair,
    y_next,
    sx_pair,
    sx_next,
    sy_pair,
    sy_next,
    velocity_new,
    displacement_grad,
):
    near, side = near_first()
    lanes = material.shape[1]
    where = lax.broadcasted_iota(jnp.int32, (rows, lanes), 0)
    for k, plane in enumerate((near, 1 - near)):
        own = pl.ds(pl.multiple_of(plane * rows, rows), rows)
        across = pl.ds(pl.multiple_of((1 - plane) * rows, rows), rows)
        occupied, density = step_factor(table, material[own])
        uphill = jnp.where(plane == 0, 0.5, -0.5)
        other, edge = (stress_near, sx_next) if k else (stress_far, sx_pair)
        moving, rest = (x_next, rest_far) if k else (sx_pair, rest_near)

        def total(slot):
            low, high = low_high(
                side,
                get_face(sy_pair, sy_pair.shape[0] - sy_next.shape[0], slot, k, lanes),
                get_face(sy_next, 0, slot, k, lanes),
            )
            value = rest[slot] + (other[slot] - edge[slot]) * uphill
            value = value - jnp.where(where == 0, low * 0.5, 0.0)
            return value + jnp.where(where == rows - 1, high * 0.5, 0.0)

        for i in range(3):
            value = velocity[i, own]
            low, high = low_high(side, y_pair[6 + i, k : k + 1], y_next[6 + i, k : k + 1])
            around = velocity[i, across] + moving[6 + i] - 6.0 * value
            for ends in (y_ends(value, low, high, rows), z_ends(value)):
                around = around + ends[0] + ends[1]
            pull = total(i) + viscosity * around
            velocity_new[i, own] = value + time_step * occupied * pull / density
            displacement_grad[i, own] = -total(3 + i)


def finish_kernel(mine, other, g_in, gb_in, g_mid, gb_mid, g_out, gb_out, small):
    count, height, _ = mine.shape
    part = height - SMALL
    total = jnp.sum(jnp.square(mine[...])) + jnp.sum(jnp.square(other[...]))
    scale = lax.rsqrt(jnp.full((1, 1), total, f32) / NPARAM + norm_eps)
    half, index = lax.rem(lax.axis_index("gy"), 2), lax.axis_index("gx")
    for m in range(count):
        for ref, side in ((mine, half), (other, 1 - half)):
            chunk = side * count + (index ^ m)
            g_mid[pl.ds(pl.multiple_of(chunk * part, part), part), :] = ref[m, :part] * scale
            small[pl.ds(pl.multiple_of(chunk * SMALL, SMALL), SMALL), :] = ref[m, part:] * scale
    g_in[...] = small[:FEAT]
    gb_in[...] = small[10:11]
    g_out[...] = small[16 : 16 + OUT]
    gb_mid[...] = small[32:34]
    gb_out[...] = small[34:35, :OUT]


def shapes(*items):
    return [jax.ShapeDtypeStruct(item, f32) for item in items]


def stay(value):
    if value.size < 2:
        return value
    return pltpu.with_memory_space_constraint(value, pltpu.HBM)


def swap_next(value, axis):
    inner = lax.axis_size(axis) - 1
    return lax.ppermute(
        value, axis, [(i, i + 1 if i % 2 else i - 1) for i in range(1, inner)]
    )


def swap(value, axis, mask):
    return lax.ppermute(value, axis, [(i, i ^ mask) for i in range(lax.axis_size(axis))])


def body(
    material,
    phase,
    clock,
    displacement,
    velocity,
    cotangent,
    material_table,
    w_in,
    b_in,
    w_mid,
    b_mid,
    w_out,
    b_out,
):
    planes, rows, lanes = material.shape
    size = planes * rows
    nx, ny = lax.axis_size("gx"), lax.axis_size("gy")
    chunks = 2 * nx
    part = 2 * HID // chunks
    face_rows = 12 * (lanes // HID)
    assert lanes % HID == 0 and ny & (ny - 1) == 0
    assert planes == 2 and chunks >= GROUPS and nx % 2 == ny % 2 == 0 and part % 8 == 0
    material = material.reshape(size, lanes)
    phase = phase.reshape(size, lanes)
    displacement = displacement.reshape(3, size, lanes)
    velocity = velocity.reshape(3, size, lanes)
    cotangent = cotangent.reshape(3, size, lanes)

    faces = pl.pallas_call(
        functools.partial(faces_kernel, rows),
        out_shape=shapes(
            (6, rows, lanes),
            (9, rows, lanes),
            *[(9, 2, lanes)] * 2,
            (2, 8, rows, lanes),
            (3, rows, lanes),
        ),
        in_specs=[HBM] * 6,
        out_specs=[VMEM] * 6,
        scratch_shapes=[
            pltpu.SMEM(material_table.shape, f32),
            *[pltpu.VMEM((size, lanes), jnp.int32)] * 2,
            *[pltpu.VMEM((3, size, lanes), f32)] * 3,
            pltpu.SemaphoreType.DMA((6,)),
        ],
        compiler_params=pltpu.CompilerParams(vmem_limit_bytes=6 << 20),
        name="faces",
    )(*map(stay, (material_table, material, phase, displacement, velocity, cotangent)))
    x_pair = swap(faces[0], "gx", 1)
    y_pair = swap(faces[2], "gy", 1)
    y_next = swap_next(faces[3], "gy")
    x_next = swap_next(faces[1], "gx")

    voxels = rows * lanes
    block = 2048
    while voxels % block:
        block //= 2
    handed = [
        ((2 * HID, HID), f32),
        ((16, HID), f32),
        ((16, HID), f32),
        ((2, HID, 128), f32),
        ((16, 128), f32),
    ]
    ready = [
        ((HID, 16), bf16),
        ((16, HID), bf16),
        ((2, HID, HID), bf16),
        ((16, HID), bf16),
        ((HID, 16), bf16),
        ((3, HID, 128), f32),
        ((2, HID, HID), bf16),
        ((16, 128), f32),
    ]
    weights = pl.pallas_call(
        weights_kernel,
        out_shape=[jax.ShapeDtypeStruct(*item) for item in ready],
        in_specs=[HBM] * 6 + [VMEM],
        out_specs=[VMEM] * 8,
        scratch_shapes=[
            pltpu.SMEM(b_out.shape, f32),
            pltpu.VMEM((FEAT, HID), bf16),
            pltpu.VMEM((1, HID), f32),
            pltpu.VMEM((2, HID), f32),
            pltpu.VMEM((OUT, HID), bf16),
            pltpu.SemaphoreType.DMA((6,)),
            pltpu.VMEM((128, HID), f32),
        ],
        compiler_params=pltpu.CompilerParams(vmem_limit_bytes=6 << 20),
        name="weights",
    )(*map(stay, (b_out, w_in.T, b_in.reshape(1, HID), b_mid, w_out, w_mid)), faces[5])

    def network(order, near):
        outs = [jax.ShapeDtypeStruct(*item) for item in handed]
        faces_out = [(6, 1, lanes)] * 2
        if order:
            outs = shapes((nx, part + SMALL, HID), (nx * (part + SMALL) + face_rows, HID))
            faces_out = [(face_rows, HID)]
        return pl.pallas_call(
            functools.partial(network_kernel, order, rows, block),
            out_shape=shapes(
                (9 - 3 * order, rows, lanes), *faces_out, (6, rows, lanes)
            )
            + outs,
            in_specs=[SMEM] + [VMEM] * len(near),
            out_specs=[VMEM] * (2 + len(faces_out) + len(outs)),
            scratch_shapes=[
                *[pltpu.VMEM((lanes // 128, 16 * rows, 128), f32)] * 2,
                *[pltpu.VMEM((16, voxels), bf16)] * 2,
                *[pltpu.VMEM((16, voxels), f32)] * 2,
                pltpu.VMEM((128, HID), f32),
                pltpu.VMEM((chunks * SMALL, HID), f32),
                *[pltpu.VMEM(*item) for item in handed[: 5 * order]],
            ],
            compiler_params=pltpu.CompilerParams(vmem_limit_bytes=36 << 20),
            cost_estimate=pl.CostEstimate(
                flops=6 * voxels * (HID * FEAT + 2 * HID * HID + OUT * HID),
                bytes_accessed=64 * voxels,
                transcendentals=3 * HID * voxels,
            ),
            name="network",
        )(clock, *near)

    first = network(0, [x_pair, y_pair, y_next, faces[4], *weights, faces[5]])
    sx_pair = swap(first[0], "gx", 1)
    second = network(1, [x_next, y_pair, y_next, faces[4], *weights, *first[1:3], *first[4:]])
    sx_next = swap_next(second[0], "gx")

    index = lax.axis_index("gx")
    sent, sx_pair = lax.optimization_barrier((second[4], sx_pair))
    sy_pair = swap(sent, "gy", 1)
    height = part + SMALL
    kept = second[3] + sy_pair[: nx * height].reshape(nx, height, HID)
    share = lax.dynamic_index_in_dim(kept, index, 0, keepdims=False)
    for m in range(1, nx):
        piece = lax.dynamic_index_in_dim(kept, index ^ m, 0, keepdims=False)
        share = share + swap(piece, "gx", m)
    share, face = lax.optimization_barrier((share, second[1]))
    sy_next = swap_next(face, "gy")
    mask = 2
    while mask < ny:
        share = share + swap(share, "gy", mask)
        if mask == 2:
            share, sx_next = lax.optimization_barrier((share, sx_next))
        mask *= 2
    share, sy_next = lax.optimization_barrier((share, sy_next))
    mine = jnp.stack([share] + [swap(share, "gx", m) for m in range(1, nx)])

    fields = pl.pallas_call(
        functools.partial(fields_kernel, rows),
        out_shape=shapes(*[(3, size, lanes)] * 2),
        in_specs=[SMEM] + [VMEM] * 13,
        out_specs=[VMEM] * 2,
        compiler_params=pltpu.CompilerParams(vmem_limit_bytes=6 << 20),
        name="fields",
    )(
        stay(material_table),
        stay(material),
        stay(velocity),
        first[0],
        second[0],
        first[3],
        second[2],
        x_next,
        y_pair,
        y_next,
        sx_pair,
        sx_next,
        sy_pair,
        sy_next,
    )
    mine, *fields = lax.optimization_barrier((mine, *fields))
    other = swap(mine, "gy", 1)
    done = pl.pallas_call(
        finish_kernel,
        out_shape=shapes((FEAT, HID), (1, HID), (2 * HID, HID), (2, HID), (OUT, HID), (1, OUT)),
        in_specs=[VMEM] * 2,
        out_specs=[VMEM] * 6,
        scratch_shapes=[pltpu.VMEM((chunks * SMALL, HID), f32)],
        compiler_params=pltpu.CompilerParams(vmem_limit_bytes=6 << 20),
        name="finish",
    )(mine, other)
    shape = (3, planes, rows, lanes)
    return (
        fields[0].reshape(shape),
        fields[1].reshape(shape),
        done[0].T,
        done[1].reshape(HID),
        done[2].reshape(2, HID, HID),
        done[3],
        done[4],
        done[5].reshape(OUT),
    )


def solution(mesh):
    in_specs = (
        P("gx", "gy", None),
        P("gx", "gy", None),
        P(),
        P(None, "gx", "gy", None),
        P(None, "gx", "gy", None),
        P(None, "gx", "gy", None),
        P(),
        P(),
        P(),
        P(),
        P(),
        P(),
        P(),
    )
    out_specs = (P(None, "gx", "gy", None), P(None, "gx", "gy", None), P(), P(), P(), P(), P(), P())
    return jax.shard_map(body, mesh=mesh, in_specs=in_specs, out_specs=out_specs, check_vma=False)
```

```python
import functools
import jax
import jax.numpy as jnp
from jax import lax
from jax.experimental import pallas as pl
from jax.experimental.pallas import tpu as pltpu
from jax.sharding import PartitionSpec as P

FEAT = 10
OUT = 9
HID = 256
PHASES = 8
NPARAM = 136713
SMALL = 8
GROUPS = 5

time_step = 0.25
viscosity = 0.2
norm_eps = 1e-06
two_pi = 6.283185307179586

bf16 = jnp.bfloat16
f32 = jnp.float32
VMEM = pl.BlockSpec(memory_space=pltpu.VMEM)
SMEM = pl.BlockSpec(memory_space=pltpu.SMEM)
HBM = pl.BlockSpec(memory_space=pltpu.HBM)


def fetch(sources, targets, sems):
    copies = [
        pltpu.make_async_copy(source, target, sems.at[k])
        for k, (source, target) in enumerate(zip(sources, targets))
    ]
    for copy in copies:
        copy.start()
    return copies


def pick(table, row, material):
    value = jnp.full(material.shape, table[row, 0], f32)
    for kind in range(1, table.shape[1]):
        value = jnp.where(material == kind, table[row, kind], value)
    return value


def step_factor(table, material):
    occupied = jnp.where(material > 0, 1.0, 0.0).astype(f32)
    return occupied, pick(table, 1, material)


def near_first():
    near = 1 - lax.rem(lax.axis_index("gx"), 2)
    return near, lax.rem(lax.axis_index("gy"), 2)


def y_ends(field, low, high, rows):
    where = lax.broadcasted_iota(jnp.int32, field.shape, 0)
    return (
        jnp.where(where == 0, low, pltpu.roll(field, 1, 0)),
        jnp.where(where == rows - 1, high, pltpu.roll(field, rows - 1, 0)),
    )


def z_ends(field):
    lanes = field.shape[1]
    where = lax.broadcasted_iota(jnp.int32, field.shape, 1)
    return (
        jnp.where(where == 0, 0.0, pltpu.roll(field, 1, 1)),
        jnp.where(where == lanes - 1, 0.0, pltpu.roll(field, lanes - 1, 1)),
    )


def half_diff(ends):
    return (ends[1] - ends[0]) * 0.5


def faces_kernel(rows, *refs):
    sources, outs, targets, sems = refs[:6], refs[6:12], refs[12:18], refs[18]
    copies = fetch(sources, targets, sems)
    near, side = near_first()
    for copy in copies:
        copy.wait()
    x_pair, x_next, y_pair, y_next, local, speed = outs
    table, material, phase, displacement, velocity, cotangent = targets
    for k, plane in enumerate((near, 1 - near)):
        own = pl.ds(pl.multiple_of(plane * rows, rows), rows)
        occupied, density = step_factor(table, material[own])
        local[k, 6] = occupied * pick(table, 0, material[own])
        local[k, 7] = two_pi * phase[own].astype(f32) / PHASES
        for i in range(3):
            carried = time_step * occupied * cotangent[i, own] / density
            moving = velocity[i, own]
            if not k:
                speed[i] = moving
            for slot, field in ((i, displacement[i, own]), (3 + i, carried), (6 + i, moving)):
                if slot < 6:
                    local[k, slot] = field
                if k:
                    x_next[slot] = field
                elif slot < 6:
                    x_pair[slot] = field
                y_pair[slot, k : k + 1] = jnp.where(side == 0, field[rows - 1 :], field[:1])
                y_next[slot, k : k + 1] = jnp.where(side == 0, field[:1], field[rows - 1 :])


def put_face(ref, base, slot, k, face):
    pieces = face.shape[1] // HID
    at = base + (2 * slot + k) * pieces
    for j in range(pieces):
        ref[at + j : at + j + 1] = face[:, j * HID : (j + 1) * HID]


def get_face(ref, base, slot, k, lanes):
    pieces = lanes // HID
    at = base + (2 * slot + k) * pieces
    return jnp.concatenate([ref[at + j : at + j + 1] for j in range(pieces)], 1)


def low_high(side, pair, following):
    return jnp.where(side == 0, following, pair), jnp.where(side == 0, pair, following)


def weights_kernel(*refs):
    sources, outs, refs = refs[:6], refs[7:15], refs[15:]
    b_out, w_inT, b_in, b_mid, w_out, sems, wide = refs
    win, winT, wmidT, wout, woutT, bias, w_mid, bias_out = outs
    for copy in fetch(sources, (b_out, w_inT, b_in, b_mid, w_out, w_mid), sems):
        copy.wait()
    rowid = lax.broadcasted_iota(jnp.int32, (16, 128), 0)
    wide[...] = jnp.zeros_like(wide)
    wide[:FEAT] = w_inT[...].astype(f32)
    winT[...] = wide[:16].astype(bf16)
    win[...] = wide[...].T[:, :16].astype(bf16)
    wide[...] = jnp.zeros_like(wide)
    wide[:OUT] = w_out[...].astype(f32)
    wout[...] = wide[:16].astype(bf16)
    woutT[...] = wide[...].T[:, :16].astype(bf16)
    for k in range(2):
        wmidT[k] = w_mid[k].astype(f32).T.astype(bf16)
    for k, row in enumerate((b_in[...], b_mid[0:1], b_mid[1:2])):
        bias[k] = jnp.broadcast_to(row, (128, HID)).T
    column = jnp.zeros((16, 128), f32)
    for k in range(OUT):
        column = jnp.where(rowid == k, b_out[k], column)
    bias_out[...] = column


def network_kernel(order, rows, block, *refs):
    clock, edge, y_pair, y_next, local, *refs = refs
    (win, winT, wmidT, wout, woutT, bias, w_mid, bias_out), refs = refs[:8], refs[8:]
    if order:
        faces_first, given, refs = refs[:2], refs[2:7], refs[7:]
        (sx, s_next, rest, kept_half, sent), refs = refs[:5], refs[5:]
    else:
        speed, sx, s_pair, s_next, rest, *refs = refs
        given, refs = refs[:5], refs[5:]
    grid_in, grid_delta, feats, delta, net, back, wide, small, *refs = refs
    near, side = near_first()
    if order:
        acc_mid, acc_in, acc_out, acc_b, acc_bo = refs
        for ref, source in zip(refs, given):
            ref[...] = source[...]
    else:
        acc_mid, acc_in, acc_out, acc_b, acc_bo = given
        for ref in given:
            ref[...] = jnp.zeros_like(ref)
    lanes = local.shape[3]
    tiles = lanes // 128
    voxels = rows * lanes
    plane = 1 - near if order else near
    strength = local[order, 6]

    def put(ref, slot, field):
        for t in range(tiles):
            ref[t, slot * rows : (slot + 1) * rows] = field[:, t * 128 : (t + 1) * 128]

    uphill = jnp.where(plane == 0, 0.5, -0.5)

    def strains(mine, other, slot):
        low, high = low_high(
            side, y_pair[slot, order : order + 1], y_next[slot, order : order + 1]
        )
        return (
            (other - edge[slot]) * uphill,
            half_diff(y_ends(mine, low, high, rows)),
            half_diff(z_ends(mine)),
        )

    for i in range(3):
        for j, value in enumerate(strains(local[order, i], local[1 - order, i], i)):
            put(grid_in, 3 * i + j, value)
        for j, value in enumerate(strains(local[order, 3 + i], local[1 - order, 3 + i], 3 + i)):
            put(grid_delta, 3 * i + j, strength * -value)
    put(grid_in, 9, jnp.sin(local[order, 7] + clock[0]))
    put(grid_in, 10, jnp.ones((rows, lanes), f32))
    for slot in range(11, 16):
        put(grid_in, slot, jnp.zeros((rows, lanes), f32))
    for slot in range(9, 16):
        put(grid_delta, slot, jnp.zeros((rows, lanes), f32))
    for r in range(rows):
        for t in range(tiles):
            at = slice((r * tiles + t) * 128, (r * tiles + t + 1) * 128)
            feats[:, at] = grid_in[t, pl.ds(r, 16, stride=rows), :].astype(bf16)
            delta[:, at] = grid_delta[t, pl.ds(r, 16, stride=rows), :].astype(bf16)

    rowid = lax.broadcasted_iota(jnp.int32, (16, 128), 0)

    def mul(a, b):
        return jnp.dot(a, b, preferred_element_type=f32)

    def mul_t(a, b):
        return lax.dot_general(a, b, (((1,), (1,)), ((), ())), preferred_element_type=f32)

    def lane_sum(value):
        total = value[:, :128].astype(f32)
        for k in range(1, block // 128):
            total = total + value[:, k * 128 : (k + 1) * 128].astype(f32)
        return total

    def slope(value):
        wider = value.astype(f32)
        return 1.0 - wider * wider

    def step(index, carry):
        at = pl.ds(pl.multiple_of(index * block, block), block)
        f, d = feats[:, at], delta[:, at]
        h1 = jnp.tanh(mul(win[...], f) + bias[0][:, :1]).astype(bf16)
        h2 = jnp.tanh(mul(w_mid[0], h1) + bias[1][:, :1]).astype(bf16)
        h3 = jnp.tanh(mul(w_mid[1], h2) + bias[2][:, :1]).astype(bf16)
        net[:, at] = mul(wout[...], h3) + bias_out[:, :1]
        acc_out[...] += mul_t(d, h3)
        acc_bo[...] += lane_sum(d)
        d3 = (mul(woutT[...], d) * slope(h3)).astype(bf16)
        acc_mid[HID:] += mul_t(d3, h2)
        acc_b[1] += lane_sum(d3)
        d2 = (mul(wmidT[1], d3) * slope(h2)).astype(bf16)
        acc_mid[:HID] += mul_t(d2, h1)
        acc_b[0] += lane_sum(d2)
        d1 = (mul(wmidT[0], d2) * slope(h1)).astype(bf16)
        acc_in[...] += mul_t(f, d1)
        back[:, at] = mul(winT[...], d1)
        return carry

    lax.fori_loop(0, voxels // block, step, 0, unroll=4)

    for r in range(rows):
        for t in range(tiles):
            at = slice((r * tiles + t) * 128, (r * tiles + t + 1) * 128)
            grid_in[t, pl.ds(r, 16, stride=rows), :] = net[:, at]
            grid_delta[t, pl.ds(r, 16, stride=rows), :] = back[:, at]

    def get(ref, slot):
        return jnp.concatenate(
            [ref[t, slot * rows : (slot + 1) * rows] for t in range(tiles)], axis=1
        )

    for base, ref, scale in ((0, grid_in, strength), (3, grid_delta, None)):
        for i in range(3):
            along = [get(ref, 3 * i + j) for j in range(3)]
            if scale is not None:
                along = [scale * item for item in along]
            slot = base + i
            sx[slot] = along[0]
            first, last = along[1][:1], along[1][rows - 1 :]
            to_pair = jnp.where(side == 0, last, first)
            to_next = jnp.where(side == 0, first, last)
            if order:
                tail = sent.shape[0] - s_next.shape[0]
                near_pair, near_next = (ref[slot] for ref in faces_first)
                put_face(sent, tail, slot, 0, near_pair)
                put_face(sent, tail, slot, 1, to_pair)
                put_face(s_next, 0, slot, 0, near_next)
                put_face(s_next, 0, slot, 1, to_next)
            else:
                s_pair[slot] = to_pair
                s_next[slot] = to_next
            rest[slot] = half_diff(y_ends(along[1], 0.0, 0.0, rows)) + half_diff(
                z_ends(along[2])
            )
    if not order:
        for i in range(3):
            sx[6 + i] = speed[i]
        return

    count = kept_half.shape[0]
    part = HID // count
    small[...] = jnp.zeros_like(small)
    small[:8] = acc_in[:8]
    small[8:16] = jnp.where(rowid[:8, :1] < 3, acc_in[8:], 0.0)
    small[16:32] = acc_out[...]
    for k in range(2):
        small[32 + k : 33 + k] = jnp.sum(acc_b[k].T, axis=0, keepdims=True)
    wide[...] = jnp.zeros_like(wide)
    wide[:16, :128] = acc_bo[...]
    small[34:35, :128] = jnp.sum(wide[:, :128].T, axis=0, keepdims=True)
    half = lax.rem(lax.axis_index("gy"), 2)
    for c in range(count):
        mine, theirs = half * count + c, (1 - half) * count + c
        kept_half[c, :part] = acc_mid[pl.ds(pl.multiple_of(mine * part, part), part)]
        kept_half[c, part:] = small[pl.ds(pl.multiple_of(mine * SMALL, SMALL), SMALL)]
        at = c * (part + SMALL)
        sent[at : at + part] = acc_mid[pl.ds(pl.multiple_of(theirs * part, part), part)]
        at += part
        sent[at : at + SMALL] = small[pl.ds(pl.multiple_of(theirs * SMALL, SMALL), SMALL)]


def fields_kernel(
    rows,
    table,
    material,
    velocity,
    stress_near,
    stress_far,
    rest_near,
    rest_far,
    x_next,
    y_pair,
    y_next,
    sx_pair,
    sx_next,
    sy_pair,
    sy_next,
    velocity_new,
    displacement_grad,
):
    near, side = near_first()
    lanes = material.shape[1]
    where = lax.broadcasted_iota(jnp.int32, (rows, lanes), 0)
    for k, plane in enumerate((near, 1 - near)):
        own = pl.ds(pl.multiple_of(plane * rows, rows), rows)
        across = pl.ds(pl.multiple_of((1 - plane) * rows, rows), rows)
        occupied, density = step_factor(table, material[own])
        uphill = jnp.where(plane == 0, 0.5, -0.5)
        other, edge = (stress_near, sx_next) if k else (stress_far, sx_pair)
        moving, rest = (x_next, rest_far) if k else (sx_pair, rest_near)

        def total(slot):
            low, high = low_high(
                side,
                get_face(sy_pair, sy_pair.shape[0] - sy_next.shape[0], slot, k, lanes),
                get_face(sy_next, 0, slot, k, lanes),
            )
            value = rest[slot] + (other[slot] - edge[slot]) * uphill
            value = value - jnp.where(where == 0, low * 0.5, 0.0)
            return value + jnp.where(where == rows - 1, high * 0.5, 0.0)

        for i in range(3):
            value = velocity[i, own]
            low, high = low_high(side, y_pair[6 + i, k : k + 1], y_next[6 + i, k : k + 1])
            around = velocity[i, across] + moving[6 + i] - 6.0 * value
            for ends in (y_ends(value, low, high, rows), z_ends(value)):
                around = around + ends[0] + ends[1]
            pull = total(i) + viscosity * around
            velocity_new[i, own] = value + time_step * occupied * pull / density
            displacement_grad[i, own] = -total(3 + i)


def finish_kernel(mine, other, g_in, gb_in, g_mid, gb_mid, g_out, gb_out, small):
    count, height, _ = mine.shape
    part = height - SMALL
    total = jnp.sum(jnp.square(mine[...])) + jnp.sum(jnp.square(other[...]))
    scale = lax.rsqrt(jnp.full((1, 1), total, f32) / NPARAM + norm_eps)
    half, index = lax.rem(lax.axis_index("gy"), 2), lax.axis_index("gx")
    for m in range(count):
        for ref, side in ((mine, half), (other, 1 - half)):
            chunk = side * count + (index ^ m)
            g_mid[pl.ds(pl.multiple_of(chunk * part, part), part), :] = ref[m, :part] * scale
            small[pl.ds(pl.multiple_of(chunk * SMALL, SMALL), SMALL), :] = ref[m, part:] * scale
    g_in[...] = small[:FEAT]
    gb_in[...] = small[10:11]
    g_out[...] = small[16 : 16 + OUT]
    gb_mid[...] = small[32:34]
    gb_out[...] = small[34:35, :OUT]


def shapes(*items):
    return [jax.ShapeDtypeStruct(item, f32) for item in items]


def stay(value):
    if value.size < 2:
        return value
    return pltpu.with_memory_space_constraint(value, pltpu.HBM)


def swap_next(value, axis):
    inner = lax.axis_size(axis) - 1
    return lax.ppermute(
        value, axis, [(i, i + 1 if i % 2 else i - 1) for i in range(1, inner)]
    )


def swap(value, axis, mask):
    return lax.ppermute(value, axis, [(i, i ^ mask) for i in range(lax.axis_size(axis))])


def body(
    material,
    phase,
    clock,
    displacement,
    velocity,
    cotangent,
    material_table,
    w_in,
    b_in,
    w_mid,
    b_mid,
    w_out,
    b_out,
):
    planes, rows, lanes = material.shape
    size = planes * rows
    nx, ny = lax.axis_size("gx"), lax.axis_size("gy")
    chunks = 2 * nx
    part = 2 * HID // chunks
    face_rows = 12 * (lanes // HID)
    assert lanes % HID == 0 and ny & (ny - 1) == 0
    assert planes == 2 and chunks >= GROUPS and nx % 2 == ny % 2 == 0 and part % 8 == 0
    material = material.reshape(size, lanes)
    phase = phase.reshape(size, lanes)
    displacement = displacement.reshape(3, size, lanes)
    velocity = velocity.reshape(3, size, lanes)
    cotangent = cotangent.reshape(3, size, lanes)

    faces = pl.pallas_call(
        functools.partial(faces_kernel, rows),
        out_shape=shapes(
            (6, rows, lanes),
            (9, rows, lanes),
            *[(9, 2, lanes)] * 2,
            (2, 8, rows, lanes),
            (3, rows, lanes),
        ),
        in_specs=[HBM] * 6,
        out_specs=[VMEM] * 6,
        scratch_shapes=[
            pltpu.SMEM(material_table.shape, f32),
            *[pltpu.VMEM((size, lanes), jnp.int32)] * 2,
            *[pltpu.VMEM((3, size, lanes), f32)] * 3,
            pltpu.SemaphoreType.DMA((6,)),
        ],
        compiler_params=pltpu.CompilerParams(vmem_limit_bytes=6 << 20),
        name="faces",
    )(*map(stay, (material_table, material, phase, displacement, velocity, cotangent)))
    x_pair = swap(faces[0], "gx", 1)
    y_pair = swap(faces[2], "gy", 1)
    y_next = swap_next(faces[3], "gy")
    x_next = swap_next(faces[1], "gx")

    voxels = rows * lanes
    block = 2048
    while voxels % block:
        block //= 2
    handed = [
        ((2 * HID, HID), f32),
        ((16, HID), f32),
        ((16, HID), f32),
        ((2, HID, 128), f32),
        ((16, 128), f32),
    ]
    ready = [
        ((HID, 16), bf16),
        ((16, HID), bf16),
        ((2, HID, HID), bf16),
        ((16, HID), bf16),
        ((HID, 16), bf16),
        ((3, HID, 128), f32),
        ((2, HID, HID), bf16),
        ((16, 128), f32),
    ]
    weights = pl.pallas_call(
        weights_kernel,
        out_shape=[jax.ShapeDtypeStruct(*item) for item in ready],
        in_specs=[HBM] * 6 + [VMEM],
        out_specs=[VMEM] * 8,
        scratch_shapes=[
            pltpu.SMEM(b_out.shape, f32),
            pltpu.VMEM((FEAT, HID), bf16),
            pltpu.VMEM((1, HID), f32),
            pltpu.VMEM((2, HID), f32),
            pltpu.VMEM((OUT, HID), bf16),
            pltpu.SemaphoreType.DMA((6,)),
            pltpu.VMEM((128, HID), f32),
        ],
        compiler_params=pltpu.CompilerParams(vmem_limit_bytes=6 << 20),
        name="weights",
    )(*map(stay, (b_out, w_in.T, b_in.reshape(1, HID), b_mid, w_out, w_mid)), faces[5])

    def network(order, near):
        outs = [jax.ShapeDtypeStruct(*item) for item in handed]
        faces_out = [(6, 1, lanes)] * 2
        if order:
            outs = shapes((nx, part + SMALL, HID), (nx * (part + SMALL) + face_rows, HID))
            faces_out = [(face_rows, HID)]
        return pl.pallas_call(
            functools.partial(network_kernel, order, rows, block),
            out_shape=shapes(
                (9 - 3 * order, rows, lanes), *faces_out, (6, rows, lanes)
            )
            + outs,
            in_specs=[SMEM] + [VMEM] * len(near),
            out_specs=[VMEM] * (2 + len(faces_out) + len(outs)),
            scratch_shapes=[
                *[pltpu.VMEM((lanes // 128, 16 * rows, 128), f32)] * 2,
                *[pltpu.VMEM((16, voxels), bf16)] * 2,
                *[pltpu.VMEM((16, voxels), f32)] * 2,
                pltpu.VMEM((128, HID), f32),
                pltpu.VMEM((chunks * SMALL, HID), f32),
                *[pltpu.VMEM(*item) for item in handed[: 5 * order]],
            ],
            compiler_params=pltpu.CompilerParams(vmem_limit_bytes=36 << 20),
            cost_estimate=pl.CostEstimate(
                flops=6 * voxels * (HID * FEAT + 2 * HID * HID + OUT * HID),
                bytes_accessed=64 * voxels,
                transcendentals=3 * HID * voxels,
            ),
            name="network",
        )(clock, *near)

    first = network(0, [x_pair, y_pair, y_next, faces[4], *weights, faces[5]])
    sx_pair = swap(first[0], "gx", 1)
    second = network(1, [x_next, y_pair, y_next, faces[4], *weights, *first[1:3], *first[4:]])
    sx_next = swap_next(second[0], "gx")

    index = lax.axis_index("gx")
    sent, sx_pair = lax.optimization_barrier((second[4], sx_pair))
    sy_pair = swap(sent, "gy", 1)
    height = part + SMALL
    kept = second[3] + sy_pair[: nx * height].reshape(nx, height, HID)
    share = lax.dynamic_index_in_dim(kept, index, 0, keepdims=False)
    for m in range(1, nx):
        piece = lax.dynamic_index_in_dim(kept, index ^ m, 0, keepdims=False)
        share = share + swap(piece, "gx", m)
    share, face = lax.optimization_barrier((share, second[1]))
    sy_next = swap_next(face, "gy")
    mask = 2
    while mask < ny:
        share = share + swap(share, "gy", mask)
        if mask == 2:
            share, sx_next = lax.optimization_barrier((share, sx_next))
        mask *= 2
    share, sy_next = lax.optimization_barrier((share, sy_next))
    mine = jnp.stack([share] + [swap(share, "gx", m) for m in range(1, nx)])

    fields = pl.pallas_call(
        functools.partial(fields_kernel, rows),
        out_shape=shapes(*[(3, size, lanes)] * 2),
        in_specs=[SMEM] + [VMEM] * 13,
        out_specs=[VMEM] * 2,
        compiler_params=pltpu.CompilerParams(vmem_limit_bytes=6 << 20),
        name="fields",
    )(
        stay(material_table),
        stay(material),
        stay(velocity),
        first[0],
        second[0],
        first[3],
        second[2],
        x_next,
        y_pair,
        y_next,
        sx_pair,
        sx_next,
        sy_pair,
        sy_next,
    )
    mine, *fields = lax.optimization_barrier((mine, *fields))
    other = swap(mine, "gy", 1)
    done = pl.pallas_call(
        finish_kernel,
        out_shape=shapes((FEAT, HID), (1, HID), (2 * HID, HID), (2, HID), (OUT, HID), (1, OUT)),
        in_specs=[VMEM] * 2,
        out_specs=[VMEM] * 6,
        scratch_shapes=[pltpu.VMEM((chunks * SMALL, HID), f32)],
        compiler_params=pltpu.CompilerParams(vmem_limit_bytes=6 << 20),
        name="finish",
    )(mine, other)
    shape = (3, planes, rows, lanes)
    return (
        fields[0].reshape(shape),
        fields[1].reshape(shape),
        done[0].T,
        done[1].reshape(HID),
        done[2].reshape(2, HID, HID),
        done[3],
        done[4],
        done[5].reshape(OUT),
    )


def solution(mesh):
    in_specs = (
        P("gx", "gy", None),
        P("gx", "gy", None),
        P(),
        P(None, "gx", "gy", None),
        P(None, "gx", "gy", None),
        P(None, "gx", "gy", None),
        P(),
        P(),
        P(),
        P(),
        P(),
        P(),
        P(),
    )
    out_specs = (P(None, "gx", "gy", None), P(None, "gx", "gy", None), P(), P(), P(), P(), P(), P())
    return jax.shard_map(body, mesh=mesh, in_specs=in_specs, out_specs=out_specs, check_vma=False)
```
